512 devices in a mesh: row: 64 (over z, y), col: 8 (over x, core).
Axes of the slice: x: 4, y: 8, z: 8, core: 2. Of those that a mesh axis runs over, the one named last changes fastest.
Arguments:
- matrix: float32 [2, 8192, 16, 1024], P(None, 'row', None, 'col'), may hold values from 0 to 32748, as said below
- pivot_rows: int32 [128], replicated, may hold values from 128 to 16383, as said below
- column_order: int32 [128], replicated, may hold values from 0 to 127, each once
- lower_inverse: int32 [128, 128], replicated, may hold values from 0 to 32748
- upper_inverse: int32 [128, 128], replicated, may hold values from 0 to 32748
Outputs:
- factored: float32 [2, 8192, 16, 1024], P(None, 'row', None, 'col')
The draws below stay inside these ranges and needn't reach their ends.
Inputs may be any that keep to these rules, and one draw needn't show every extreme that they name: `matrix`: every entry is a whole number. `pivot_rows`: 128 distinct rows, none of them below 128; 128 and 16383 are always among them.
All inputs are finite; a program needn't handle non-finite values.
Results may differ from the reference program's by a relative error of at most 0.0003.
Values sent between devices are 32-bit elements; how exact they have to be, the bound alone decides.
A program may use at most 64 MiB of HBM per device.

```python
import jax
import jax.numpy as jnp
from jax import lax

NB = 128
RCY = 2
N = 16384
CCY = 16
N_ROW = 64
N_COL = 8


def draw_matrix(key, part):
    return jax.random.randint(key, (RCY, N_ROW * NB, CCY, N_COL * NB), 0, 32749).astype(jnp.float32)


def draw_pivot_rows(key, part):
    inner_key = jax.random.fold_in(key, 11)
    order_key = jax.random.fold_in(key, 12)
    middle = 1 + jax.random.permutation(inner_key, N - NB - 2)[:NB - 2]
    chosen = jnp.concatenate([jnp.array([0, N - NB - 1], jnp.int32), middle.astype(jnp.int32)]) + NB
    return jax.random.permutation(order_key, chosen).astype(jnp.int32)


def touch_ends(values, rng, least, top_value):
    extent = values.shape
    index_at = [jax.random.randint(jax.random.fold_in(rng, axis), (), 0, extent[axis]) for axis in range(len(extent))]
    values = values.at[tuple(index_at)].set(least)
    longest = extent.index(max(extent))
    index_at[longest] = (index_at[longest] + 1) % extent[longest]
    return values.at[tuple(index_at)].set(top_value)


def setup_inputs(seed: int = 0) -> dict:
    key_list = jax.random.split(jax.random.key(seed), 6)
    matrix = draw_matrix(jax.random.fold_in(key_list[5], 71), 0)
    pivot_rows = draw_pivot_rows(jax.random.fold_in(key_list[5], 71), 0)
    column_order = jax.random.permutation(key_list[2], NB).astype(jnp.int32)
    lower_inverse = touch_ends(jax.random.randint(key_list[3], (NB, NB), 0, 32749), jax.random.fold_in(key_list[3], 1), 0, 32748).astype(jnp.int32)
    upper_inverse = touch_ends(jax.random.randint(key_list[4], (NB, NB), 0, 32749), jax.random.fold_in(key_list[4], 1), 0, 32748).astype(jnp.int32)
    return {"matrix": matrix, "pivot_rows": pivot_rows, "column_order": column_order, "lower_inverse": lower_inverse, "upper_inverse": upper_inverse}


prime_modulus = 32749
limb_divisors = (1, 32, 1024)


def split_limbs(values):
    return [((values // divisor) % 32).astype(jnp.bfloat16) for divisor in limb_divisors]


def modular_product(left_side, right_side):
    left_limbs = split_limbs(left_side.astype(jnp.int32))
    right_limbs = split_limbs(right_side.astype(jnp.int32))
    outcome = jnp.zeros((left_side.shape[0], right_side.shape[1]), jnp.int32)
    factor = 1
    for degree in range(5):
        limb_pairs = [(left_degree, degree - left_degree) for left_degree in range(3) if 0 <= degree - left_degree < 3]
        stacked_left = jnp.concatenate([left_limbs[limb_pair[0]] for limb_pair in limb_pairs], axis=1)
        stacked_right = jnp.concatenate([right_limbs[limb_pair[1]] for limb_pair in limb_pairs], axis=0)
        partial_sum = jnp.dot(stacked_left, stacked_right, preferred_element_type=jnp.float32).astype(jnp.int32)
        outcome = (outcome + (partial_sum % prime_modulus) * factor % prime_modulus) % prime_modulus
        factor = factor * 32 % prime_modulus
    return outcome


def reference(matrix, pivot_rows, column_order, lower_inverse, upper_inverse):
    whole = matrix.reshape(N, N)
    swapped = whole.at[:NB].set(whole[pivot_rows]).at[pivot_rows].set(whole[:NB])
    swapped = swapped.at[:, :NB].set(swapped[:, column_order])
    upper_block = modular_product(lower_inverse, swapped[:NB])
    lower_block = modular_product(swapped[NB:, :NB], upper_inverse)
    upper_right = upper_block[:, NB:]

    def block_update(row_block):
        return modular_product(row_block, upper_right)

    update = lax.map(block_update, lower_block.reshape((N - NB) // NB, NB, NB)).reshape(N - NB, N - NB)
    trailing = (swapped[NB:, NB:].astype(jnp.int32) - update) % prime_modulus
    result = jnp.concatenate([upper_block, jnp.concatenate([lower_block, trailing], axis=1)], axis=0)
    return result.astype(jnp.float32).reshape(RCY, N_ROW * NB, CCY, N_COL * NB)
```

```python
import jax
import jax.numpy as jnp
from jax import lax
from jax.experimental import pallas as pl
from jax.experimental.pallas import tpu as pltpu
from jax.sharding import PartitionSpec as P

prime_modulus = 32749
limb_divisors = (1, 32, 1024)
PF = 32749.0
INV = 1.0 / 32749.0
MESH = pl.DeviceIdType.MESH
F32 = jnp.float32
BF16 = jnp.bfloat16
I32 = jnp.int32


def sum_over(array, axis):
    count = lax.axis_size(axis)
    step = 1
    while step < count:
        array = array + lax.ppermute(array, axis, [(i, i ^ step) for i in range(count)])
        step *= 2
    return array


def split_limbs(values):
    return [(values // divisor % 32).astype(jnp.bfloat16) for divisor in limb_divisors]


def modular_product(left_side, right_side):
    left_limbs = split_limbs(left_side.astype(jnp.int32))
    right_limbs = split_limbs(right_side.astype(jnp.int32))
    outcome = jnp.zeros((left_side.shape[0], right_side.shape[1]), jnp.int32)
    factor = 1
    for degree in range(5):
        limb_pairs = [
            (left_degree, degree - left_degree)
            for left_degree in range(3)
            if 0 <= degree - left_degree < 3
        ]
        stacked_left = jnp.concatenate(
            [left_limbs[limb_pair[0]] for limb_pair in limb_pairs], axis=1
        )
        stacked_right = jnp.concatenate(
            [right_limbs[limb_pair[1]] for limb_pair in limb_pairs], axis=0
        )
        partial_sum = jnp.dot(
            stacked_left, stacked_right, preferred_element_type=jnp.float32
        ).astype(jnp.int32)
        outcome = (outcome + partial_sum % prime_modulus * factor % prime_modulus) % prime_modulus
        factor = factor * 32 % prime_modulus
    return outcome


def general_path(matrix, pivot_rows, column_order, lower_inverse, upper_inverse):
    row_cycles = matrix.shape[0]
    panel_width = matrix.shape[1]
    col_cycles = matrix.shape[2]
    local_rows = row_cycles * panel_width
    local_cols = col_cycles * panel_width
    row_count = lax.axis_size("row")
    row_rank = lax.axis_index("row")
    col_rank = lax.axis_index("col")
    flat = matrix.reshape(local_rows, local_cols)
    stride = row_count * panel_width
    owner = pivot_rows % stride // panel_width
    local_slot = pivot_rows // stride * panel_width + pivot_rows % panel_width
    owned = owner == row_rank
    picked = jnp.where(owned[:, None], flat[jnp.where(owned, local_slot, 0)], 0.0)
    top_rows = jnp.where(row_rank == 0, flat[:panel_width], 0.0)
    new_top, old_top = sum_over(picked, "row"), sum_over(top_rows, "row")
    upper_all = modular_product(lower_inverse, new_top)
    targets = jnp.where(owned, local_slot, local_rows)
    swapped = flat.at[targets].set(old_top, mode="drop")
    panel = swapped[:, :panel_width][:, column_order]
    panel_all = sum_over(jnp.where(col_rank == 0, panel, 0.0), "col")
    lower_all = modular_product(panel_all, upper_inverse)
    permuted = upper_all.at[:, :panel_width].set(upper_all[:, column_order])
    upper_use = jnp.where(col_rank == 0, permuted, upper_all)
    update = modular_product(lower_all, upper_use)
    result = (swapped.astype(jnp.int32) - update) % prime_modulus
    result = result.at[:, :panel_width].set(
        jnp.where(col_rank == 0, lower_all, result[:, :panel_width])
    )
    result = result.at[:panel_width].set(jnp.where(row_rank == 0, upper_use, result[:panel_width]))
    return result.astype(jnp.float32).reshape(row_cycles, panel_width, col_cycles, panel_width)


R_T1, R_T2, R_T3, R_O1, R_O2, R_O3, R_TV, R_OK = 0, 2, 4, 6, 8, 10, 12, 14


def table_kernel(rank_ref, pivots_ref, out_ref):
    me = rank_ref[0]
    my_z, my_y = me >> 3, me & 7
    sub = lax.broadcasted_iota(I32, (128, 128), 0)
    lane = lax.broadcasted_iota(I32, (128, 128), 1)
    eye = sub == lane
    t = lax.broadcasted_iota(I32, (1, 128), 1)
    pivots = pivots_ref[...]

    def column(row):
        return jnp.sum(jnp.where(eye, row.astype(F32), 0.0), axis=1, keepdims=True)

    owner = (pivots & 8191) >> 7
    slot_col = column(((pivots >> 13) << 7) | (pivots & 127))
    index_col = lax.broadcasted_iota(I32, (128, 1), 0).astype(F32)
    good = jnp.ones((1, 128), jnp.bool_)
    out_ref[...] = jnp.zeros_like(out_ref)
    for c in range(2):
        if c == 0:
            key, plane, minor = owner, my_z, my_y
        else:
            key, plane, minor = ((owner & 7) << 3) | (owner >> 3), my_y, my_z
        key_col = column(key)
        full_row = (key * 128 + t).astype(F32)
        full_col = key_col * 128.0 + index_col
        rank_col = jnp.sum(jnp.where(full_row < full_col, 1.0, 0.0), axis=1, keepdims=True)

        def before(x):
            return jnp.sum(
                jnp.where(key_col < x.astype(F32), 1.0, 0.0), axis=0, keepdims=True
            ).astype(I32)

        def at_rank(values_col, s):
            return jnp.sum(
                jnp.where(rank_col == s.astype(F32), values_col, 0.0), axis=0, keepdims=True
            ).astype(I32)

        def first(start, residue):
            return start + ((residue - start) & 7)

        zero = jnp.zeros((1, 128), I32)
        half, odd = t >> 1, t & 1
        mine = zero + (plane * 8 + minor)
        start = before(mine)
        end = before(mine + 1)
        s = first(start, half) + 8 * odd
        slot = at_rank(slot_col, s)
        held = (s < end) & (t < 16)
        out_ref[R_T1 + c:R_T1 + c + 1, :] = jnp.where(held, slot, 0)
        out_ref[R_TV + c:R_TV + c + 1, :] = jnp.where(held, slot, -1)

        plane_start = before(zero + plane * 8)
        my_first = first(plane_start, minor)
        s = my_first + 8 * t
        key_s = at_rank(key_col, s)
        start = before(key_s)
        where_n2 = (key_s & 7) * 2 + ((s - first(start, minor)) >> 3)
        out_ref[R_T2 + c:R_T2 + c + 1, :] = jnp.clip(where_n2, 0, 15)

        s = 8 * t + minor
        plane_s = at_rank(key_col, s) >> 3
        place = plane_s * 4 + ((s - first(before(plane_s * 8), minor)) >> 3)
        out_ref[R_T3 + c:R_T3 + c + 1, :] = jnp.clip(place, 0, 31)

        s = 8 * (t & 15) + (t >> 4)
        out_ref[R_O1 + c:R_O1 + c + 1, :] = at_rank(index_col, s)

        s = first(before((t >> 2) * 8), minor) + 8 * (t & 3)
        out_ref[R_O2 + c:R_O2 + c + 1, :] = jnp.clip((s - minor) >> 3, 0, 15)

        s = first(before(zero + plane * 8 + half), minor) + 8 * odd
        out_ref[R_O3 + c:R_O3 + c + 1, :] = jnp.clip((s - my_first) >> 3, 0, 3)

        if c == 0:
            good = good & (before(t + 1) - before(t) <= 16)
        good = good & (before(t * 8 + 8) - before(t * 8) <= 32)
    worst = jnp.min(jnp.where(good, 1.0, 0.0), axis=1, keepdims=True)
    out_ref[R_OK:R_OK + 1, :] = jnp.broadcast_to(worst, (1, 128)).astype(I32)


def make_tables(row_rank, pivot_rows):
    return pl.pallas_call(
        table_kernel,
        name="tables",
        out_shape=jax.ShapeDtypeStruct((16, 128), I32),
        in_specs=[
            pl.BlockSpec(memory_space=pltpu.SMEM),
            pl.BlockSpec(memory_space=pltpu.VMEM),
        ],
        out_specs=pl.BlockSpec(memory_space=pltpu.VMEM),
    )(row_rank.reshape(1), pivot_rows.reshape(1, 128))


def exchange_kernel(
    tab, mat, new_out, old_out, pan_out, opan_out,
    n1s, n1r, n2s, n2r, o1s, o1r, o2s, o2r, o3s,
    n1_ss, n1_rs, n2_ss, n2_rs, n3_ss, n3_rs, o1_ss, o1_rs, o2_ss, o2_rs, o3_ss, o3_rs,
    p1_ss, p1_rs, p2_ss, p2_rs,
):
    rank = lax.axis_index("row")
    col = lax.axis_index("col")
    z, y = rank // 8, rank % 8
    coords = ((z, y), (y, z))

    def row_of(c, plane, minor):
        return plane * 8 + minor if c == 0 else minor * 8 + plane

    def minor_peer(c, step):
        plane, minor = coords[c]
        other = (minor + step) % 8
        return other, (row_of(c, plane, other), col)

    def plane_peer(c, step):
        plane, minor = coords[c]
        other = (plane + step) % 8
        return other, (row_of(c, other, minor), col)

    def col_peer(step):
        return (rank, (col + step) % 8)

    def copy(src, dst, ssem, rsem, dev):
        return pltpu.make_async_remote_copy(
            src_ref=src, dst_ref=dst, send_sem=ssem, recv_sem=rsem,
            device_id=dev, device_id_type=MESH,
        )

    new2d = new_out.reshape(2 * 8 * 128, 128)

    barrier = pltpu.get_barrier_semaphore()
    for step in range(1, 8):
        for dev in (minor_peer(0, step)[1], minor_peer(1, step)[1], col_peer(step)):
            pl.semaphore_signal(barrier, inc=1, device_id=dev, device_id_type=MESH)

    def mat_tile(row, c):
        return mat[row * 2 + c]

    for c in range(2):
        for k in range(16):
            n1s[c, k] = mat_tile(tab[R_T1 + c, k], c)

    @pl.when(col == 0)
    def _():
        pan_out[...] = mat.reshape(4096, 128)[pl.ds(0, 256, stride=16), :]

    @pl.when(rank == 0)
    def _():
        for c in range(2):
            def body(u, carry):
                o1s[c, u] = mat_tile(tab[R_O1 + c, u], c)
                return carry
            lax.fori_loop(0, 128, body, 0)

    pl.semaphore_wait(barrier, 21)

    n1 = []
    for step in range(1, 8):
        for c in range(2):
            other, dev = minor_peer(c, step)
            minor = coords[c][1]
            d = copy(n1s.at[c, pl.ds(2 * other, 2)], n1r.at[c, pl.ds(2 * minor, 2)],
                     n1_ss.at[c, step], n1_rs.at[c, step], dev)
            d.start()
            n1.append(d)

    p1 = []
    for step in range(1, 8):
        p1.append(copy(pan_out, pan_out, p1_ss.at[step], p1_rs, (rank, step)))

    @pl.when(col == 0)
    def _():
        for d in p1:
            d.start()

    o1 = []
    for step in (1, 7, 2, 6, 3, 5, 4):
        for c in range(2):
            dev = (step if c == 0 else step * 8, col)
            o1.append(copy(o1s.at[c, pl.ds(16 * step, 16)], o1r.at[c],
                           o1_ss.at[c, step], o1_rs.at[c], dev))

    @pl.when(rank == 0)
    def _():
        for d in o1:
            d.start()
        for c in range(2):
            o1r[c] = o1s[c, pl.ds(0, 16)]

    for c in range(2):
        minor = coords[c][1]
        n1r[c, pl.ds(2 * minor, 2)] = n1s[c, pl.ds(2 * minor, 2)]

    for d in n1:
        d.wait_recv()

    n2 = []
    for c in range(2):
        plane = coords[c][0]
        for j in range(4):
            row = n1r[c, tab[R_T2 + c, j]]
            n2s[c, j] = row
            n2r[c, plane * 4 + j] = row
    for step in range(1, 8):
        for c in range(2):
            plane = coords[c][0]
            other, dev = plane_peer(c, step)
            d = copy(n2s.at[c], n2r.at[c, pl.ds(4 * plane, 4)],
                     n2_ss.at[c, step], n2_rs.at[c, step], dev)
            d.start()
            n2.append(d)

    o2 = [[], []]
    for c in range(2):
        plane, minor = coords[c]
        for step in (1, 7, 2, 6, 3, 5, 4):
            dev = (row_of(c, step, minor), col)
            o2[c].append(copy(o2s.at[c, pl.ds(4 * step, 4)], o2r.at[c],
                              o2_ss.at[c, step], o2_rs.at[c], dev))

    def do_o2():
        for c in range(2):
            plane, minor = coords[c]

            @pl.when((plane == 0) & (minor != 0))
            def _():
                copy(o1s.at[c, pl.ds(0, 16)], o1r.at[c], o1_ss.at[c, 0], o1_rs.at[c],
                     (0, col)).wait_recv()

            @pl.when(plane == 0)
            def _():
                def body(v, carry):
                    o2s[c, v] = o1r[c, tab[R_O2 + c, v]]
                    return carry
                lax.fori_loop(0, 32, body, 0)
                for d in o2[c]:
                    d.start()
                o2r[c] = o2s[c, pl.ds(0, 4)]

    for d in n2:
        d.wait_recv()

    for c in range(2):
        minor = coords[c][1]
        for k in range(16):
            row = n2r[c, tab[R_T3 + c, k]]
            new2d[pl.ds(c * 1024 + minor * 16 + k, 8, stride=128), :] = row

    sends = []

    def hop_copies(h):
        found = []
        for q in range(2):
            for c in range(2):
                minor = coords[c][1]
                for way in range(2):
                    if h == 4 and q != way:
                        continue
                    sign = 1 if way == 0 else -1
                    block = (minor - sign * (h - 1)) % 8
                    part = new_out.at[c, pl.ds(4 * q, 4), pl.ds(pl.multiple_of(16 * block, 16), 16), :]
                    found.append(copy(part, part, n3_ss.at[c, h, way, q], n3_rs.at[c, h, way, q],
                                      minor_peer(c, sign)[1]))
        return found

    hops = {h: hop_copies(h) for h in range(1, 5)}

    def key(h):
        return [(q, c, way) for q in range(2) for c in range(2) for way in range(2)
                if not (h == 4 and q != way)]

    for d in hops[1]:
        d.start()
    do_o2()
    for h in range(2, 5):
        before = dict(zip(key(h - 1), hops[h - 1]))
        now = dict(zip(key(h), hops[h]))
        for k in key(h - 1):
            before[k].wait_recv()
            if k in now:
                now[k].start()
        if h == 2:
            o3 = []
            for c in range(2):
                @pl.when(coords[c][0] != 0)
                def _():
                    o2[c][0].wait_recv()

            for c in range(2):
                minor = coords[c][1]
                for k in range(16):
                    o3s[c, k] = o2r[c, tab[R_O3 + c, k]]
                old_out[c, pl.ds(2 * minor, 2)] = o3s[c, pl.ds(2 * minor, 2)]
                for step in range(1, 8):
                    other, dev = minor_peer(c, step)
                    d = copy(o3s.at[c, pl.ds(2 * other, 2)], old_out.at[c, pl.ds(2 * minor, 2)],
                             o3_ss.at[c, step], o3_rs.at[c, step], dev)
                    d.start()
                    o3.append(d)
    for d in o3:
        d.wait_recv()
    p2 = []
    for step in range(1, 8):
        p2.append(copy(opan_out, opan_out, p2_ss.at[step], p2_rs, (rank, step)))

    @pl.when(col == 0)
    def _():
        for k in range(16):
            opan_out[k:k + 1, :] = old_out[0, k, 0:1, :]
        for d in p2:
            d.start()

    for d in hops[4]:
        d.wait_recv()

    @pl.when(col != 0)
    def _():
        p1[0].wait_recv()
        p2[0].wait_recv()

    for d in n1 + n2 + o3 + [d for h in hops for d in hops[h]]:
        d.wait_send()

    @pl.when(rank == 0)
    def _():
        for d in o1:
            d.wait_send()

    for c in range(2):
        @pl.when(coords[c][0] == 0)
        def _():
            for d in o2[c]:
                d.wait_send()

    @pl.when(col == 0)
    def _():
        for d in p1 + p2:
            d.wait_send()


def exchange(tables, mat):
    vmem = pl.BlockSpec(memory_space=pltpu.VMEM)
    dma = pltpu.SemaphoreType.DMA
    tile = lambda *lead: pltpu.VMEM((*lead, 8, 128), F32)
    return pl.pallas_call(
        exchange_kernel,
        name="exchange",
        out_shape=(
            jax.ShapeDtypeStruct((2, 8, 128, 128), F32),
            jax.ShapeDtypeStruct((2, 16, 8, 128), F32),
            jax.ShapeDtypeStruct((256, 128), F32),
            jax.ShapeDtypeStruct((16, 128), F32),
        ),
        in_specs=[pl.BlockSpec(memory_space=pltpu.SMEM), vmem],
        out_specs=(vmem,) * 4,
        scratch_shapes=[
            tile(2, 16), tile(2, 16), tile(2, 4), tile(2, 32), tile(2, 128), tile(2, 16),
            tile(2, 32), tile(2, 4), tile(2, 16),
            dma((2, 8)), dma((2, 8)), dma((2, 8)), dma((2, 8)),
            dma((2, 5, 2, 2)), dma((2, 5, 2, 2)),
            dma((2, 8)), dma((2,)), dma((2, 8)), dma((2,)), dma((2, 8)), dma((2, 8)),
            dma((8,)), dma, dma((8,)), dma,
        ],
        compiler_params=pltpu.CompilerParams(collective_id=0, has_side_effects=True),
    )(tables, mat)


def centred(x):
    return x - PF * jnp.floor(x * INV + 0.5)


def scaled_digits(a):
    a = centred(a)
    b = centred(a * 256.0)
    both = jnp.concatenate([b, a], axis=1)
    high = jnp.floor(both * (1.0 / 128.0) + 0.5)
    return jnp.concatenate([high, both - 128.0 * high], axis=0).astype(BF16)


def plain_digits(x):
    high = jnp.floor(x * (1.0 / 256.0) + 0.5)
    return jnp.concatenate([high.astype(BF16), (x - 256.0 * high).astype(BF16)], axis=0)


def product(left, right):
    both = jnp.dot(left, right, preferred_element_type=F32)
    rows = both.shape[0] // 2
    return centred(both[:rows]) * 128.0 + both[rows:]


def one_hot_columns(values, hot):
    high = jnp.floor(values * (1.0 / 256.0))
    low = values - 256.0 * high
    return 256.0 * jnp.dot(high.astype(BF16), hot, preferred_element_type=F32) + jnp.dot(
        low.astype(BF16), hot, preferred_element_type=F32
    )


def compute_kernel(
    tab, tabv, new_ref, old_ref, pan_ref, opan_ref, order_ref, linv_ref, uinv_ref, mat_hbm,
    out_ref, mat, pan, low, linv_d, low_d, sem,
):
    rank, col = lax.axis_index("row"), lax.axis_index("col")
    fetch = pltpu.make_async_copy(mat_hbm, mat, sem)
    fetch.start()
    sub = lax.broadcasted_iota(I32, (128, 128), 0)
    eye = sub == lax.broadcasted_iota(I32, (128, 128), 1)

    pan[...] = pan_ref[...]

    def patch_panel(k, carry):
        slot = tab[R_TV, k]

        @pl.when(slot >= 0)
        def _():
            pan[pl.ds(slot, 1), :] = opan_ref[pl.ds(k, 1), :]
        return carry
    lax.fori_loop(0, 16, patch_panel, 0)

    order_hot = (sub == order_ref[...]).astype(BF16)
    uinv = uinv_ref[...].astype(F32)
    u_high = jnp.floor(uinv * (1.0 / 256.0))
    u_low = uinv - 256.0 * u_high
    uperm = 256.0 * jnp.dot(order_hot, u_high.astype(BF16), preferred_element_type=F32) + jnp.dot(
        order_hot, u_low.astype(BF16), preferred_element_type=F32
    )
    lower = centred(product(scaled_digits(pan[...]), plain_digits(centred(uperm))))
    low[...] = jnp.where(lower < 0.0, lower + PF, lower)
    top = jnp.where(rank == 0, jnp.where(eye, -1.0, 0.0), lower[:128])
    low_d[...] = scaled_digits(jnp.concatenate([top, lower[128:]], axis=0))

    linv = linv_ref[...].astype(F32)
    for c in range(2):
        hot = (sub == tabv[R_O1 + c:R_O1 + c + 1, :]).astype(BF16)
        linv_d[c] = scaled_digits(one_hot_columns(linv, hot))

    fetch.wait()

    def patch_rows(k, carry):
        for c in range(2):
            slot = tab[R_TV + c, k]

            @pl.when(slot >= 0)
            def _():
                mat[pl.ds(pl.multiple_of(slot * 16 + 8 * c, 8), 8), :] = old_ref[c, k]
        return carry
    lax.fori_loop(0, 16, patch_rows, 0)

    @pl.when(rank == 0)
    def _():
        mat[0:2048, :] = jnp.zeros((2048, 128), F32)

    first_upper = None
    for pair in range(8):
        c, e = pair // 4, (pair % 4) * 2
        x = jnp.concatenate([new_ref[c, e], new_ref[c, e + 1]], axis=1)
        upper = centred(product(linv_d[c], plain_digits(x)))
        if pair == 0:
            first_upper = upper[:, :128]
        update = product(low_d[...], plain_digits(upper))
        for side in range(2):
            rows = pl.ds(2 * pair + side, 256, stride=16)
            value = mat[rows, :] - update[:, 128 * side:128 * side + 128]
            out_ref[rows, :] = value - PF * jnp.floor((value + 0.5) * INV)

    @pl.when(col == 0)
    def _():
        out_ref[pl.ds(0, 256, stride=16), :] = low[...]

        @pl.when(rank == 0)
        def _():
            upper = jnp.where(first_upper < 0.0, first_upper + PF, first_upper)
            out_ref[pl.ds(0, 128, stride=16), :] = one_hot_columns(upper, order_hot)


def compute(tables, new, old, panel, old_panel, column_order, linv, uinv, mat):
    vmem = pl.BlockSpec(memory_space=pltpu.VMEM)
    smem = pl.BlockSpec(memory_space=pltpu.SMEM)
    return pl.pallas_call(
        compute_kernel,
        name="update",
        out_shape=jax.ShapeDtypeStruct((4096, 128), F32),
        in_specs=[smem] + [vmem] * 8 + [pl.BlockSpec(memory_space=pl.ANY)],
        out_specs=vmem,
        scratch_shapes=[
            pltpu.VMEM((4096, 128), F32),
            pltpu.VMEM((256, 128), F32),
            pltpu.VMEM((256, 128), F32),
            pltpu.VMEM((2, 256, 256), BF16),
            pltpu.VMEM((512, 256), BF16),
            pltpu.SemaphoreType.DMA,
        ],
    )(tables, tables, new, old, panel, old_panel, column_order, linv, uinv, mat)


def fast_path(tables, matrix, column_order, lower_inverse, upper_inverse):
    mat = matrix.reshape(4096, 128)
    new, old, panel, old_panel = exchange(tables, matrix.reshape(512, 8, 128))
    out = compute(tables, new, old, panel, old_panel, column_order.reshape(1, 128),
                  lower_inverse, upper_inverse, mat)
    return out.reshape(matrix.shape)


def on_device(matrix, pivot_rows, column_order, lower_inverse, upper_inverse):
    tables = make_tables(lax.axis_index("row"), pivot_rows)
    return lax.cond(
        tables[R_OK, 0] > 0,
        lambda: fast_path(tables, matrix, column_order, lower_inverse, upper_inverse),
        lambda: general_path(matrix, pivot_rows, column_order, lower_inverse, upper_inverse),
    )


def solution(mesh):
    return jax.shard_map(
        on_device,
        mesh=mesh,
        in_specs=(P(None, "row", None, "col"), P(), P(), P(), P()),
        out_specs=P(None, "row", None, "col"),
        check_vma=False,
    )
```

```python
import jax
import jax.numpy as jnp
from jax import lax
from jax.experimental import pallas as pl
from jax.experimental.pallas import tpu as pltpu
from jax.sharding import PartitionSpec as P

prime_modulus = 32749
limb_divisors = (1, 32, 1024)
PF = 32749.0
INV = 1.0 / 32749.0
MESH = pl.DeviceIdType.MESH
F32 = jnp.float32
BF16 = jnp.bfloat16
I32 = jnp.int32


def sum_over(array, axis):
    count = lax.axis_size(axis)
    step = 1
    while step < count:
        array = array + lax.ppermute(array, axis, [(i, i ^ step) for i in range(count)])
        step *= 2
    return array


def split_limbs(values):
    return [(values // divisor % 32).astype(jnp.bfloat16) for divisor in limb_divisors]


def modular_product(left_side, right_side):
    left_limbs = split_limbs(left_side.astype(jnp.int32))
    right_limbs = split_limbs(right_side.astype(jnp.int32))
    outcome = jnp.zeros((left_side.shape[0], right_side.shape[1]), jnp.int32)
    factor = 1
    for degree in range(5):
        limb_pairs = [
            (left_degree, degree - left_degree)
            for left_degree in range(3)
            if 0 <= degree - left_degree < 3
        ]
        stacked_left = jnp.concatenate(
            [left_limbs[limb_pair[0]] for limb_pair in limb_pairs], axis=1
        )
        stacked_right = jnp.concatenate(
            [right_limbs[limb_pair[1]] for limb_pair in limb_pairs], axis=0
        )
        partial_sum = jnp.dot(
            stacked_left, stacked_right, preferred_element_type=jnp.float32
        ).astype(jnp.int32)
        outcome = (outcome + partial_sum % prime_modulus * factor % prime_modulus) % prime_modulus
        factor = factor * 32 % prime_modulus
    return outcome


def general_path(matrix, pivot_rows, column_order, lower_inverse, upper_inverse):
    row_cycles = matrix.shape[0]
    panel_width = matrix.shape[1]
    col_cycles = matrix.shape[2]
    local_rows = row_cycles * panel_width
    local_cols = col_cycles * panel_width
    row_count = lax.axis_size("row")
    row_rank = lax.axis_index("row")
    col_rank = lax.axis_index("col")
    flat = matrix.reshape(local_rows, local_cols)
    stride = row_count * panel_width
    owner = pivot_rows % stride // panel_width
    local_slot = pivot_rows // stride * panel_width + pivot_rows % panel_width
    owned = owner == row_rank
    picked = jnp.where(owned[:, None], flat[jnp.where(owned, local_slot, 0)], 0.0)
    top_rows = jnp.where(row_rank == 0, flat[:panel_width], 0.0)
    new_top, old_top = sum_over(picked, "row"), sum_over(top_rows, "row")
    upper_all = modular_product(lower_inverse, new_top)
    targets = jnp.where(owned, local_slot, local_rows)
    swapped = flat.at[targets].set(old_top, mode="drop")
    panel = swapped[:, :panel_width][:, column_order]
    panel_all = sum_over(jnp.where(col_rank == 0, panel, 0.0), "col")
    lower_all = modular_product(panel_all, upper_inverse)
    permuted = upper_all.at[:, :panel_width].set(upper_all[:, column_order])
    upper_use = jnp.where(col_rank == 0, permuted, upper_all)
    update = modular_product(lower_all, upper_use)
    result = (swapped.astype(jnp.int32) - update) % prime_modulus
    result = result.at[:, :panel_width].set(
        jnp.where(col_rank == 0, lower_all, result[:, :panel_width])
    )
    result = result.at[:panel_width].set(jnp.where(row_rank == 0, upper_use, result[:panel_width]))
    return result.astype(jnp.float32).reshape(row_cycles, panel_width, col_cycles, panel_width)


def centred(x):
    return x - PF * jnp.floor(x * INV + 0.5)


def scaled_digits(a):
    a = centred(a)
    b = centred(a * 256.0)
    both = jnp.concatenate([b, a], axis=1)
    high = jnp.floor(both * (1.0 / 128.0) + 0.5)
    return jnp.concatenate([high, both - 128.0 * high], axis=0).astype(BF16)


def plain_digits(x):
    high = jnp.floor(x * (1.0 / 256.0) + 0.5)
    return jnp.concatenate([high.astype(BF16), (x - 256.0 * high).astype(BF16)], axis=0)


def product(left, right):
    both = jnp.dot(left, right, preferred_element_type=F32)
    rows = both.shape[0] // 2
    return centred(both[:rows]) * 128.0 + both[rows:]


def one_hot_columns(values, hot):
    high = jnp.floor(values * (1.0 / 256.0))
    low = values - 256.0 * high
    return 256.0 * jnp.dot(high.astype(BF16), hot, preferred_element_type=F32) + jnp.dot(
        low.astype(BF16), hot, preferred_element_type=F32
    )


R_T1, R_T2, R_T3, R_O1, R_O2, R_O3, R_TV, R_OK = 0, 2, 4, 6, 8, 10, 12, 14


def fill_tables(my_z, my_y, pivots_ref, out_ref):
    sub = lax.broadcasted_iota(I32, (128, 128), 0)
    lane = lax.broadcasted_iota(I32, (128, 128), 1)
    eye = sub == lane
    t = lax.broadcasted_iota(I32, (1, 128), 1)
    pivots = pivots_ref[...]

    def column(row):
        return jnp.sum(jnp.where(eye, row.astype(F32), 0.0), axis=1, keepdims=True)

    owner = (pivots & 8191) >> 7
    slot_col = column(((pivots >> 13) << 7) | (pivots & 127))
    index_col = lax.broadcasted_iota(I32, (128, 1), 0).astype(F32)
    good = jnp.ones((1, 128), jnp.bool_)
    out_ref[...] = jnp.zeros_like(out_ref)
    for c in range(2):
        if c == 0:
            key, plane, minor = owner, my_z, my_y
        else:
            key, plane, minor = ((owner & 7) << 3) | (owner >> 3), my_y, my_z
        key_col = column(key)
        full_row = (key * 128 + t).astype(F32)
        full_col = key_col * 128.0 + index_col
        rank_col = jnp.sum(jnp.where(full_row < full_col, 1.0, 0.0), axis=1, keepdims=True)

        def before(x):
            return jnp.sum(
                jnp.where(key_col < x.astype(F32), 1.0, 0.0), axis=0, keepdims=True
            ).astype(I32)

        def at_rank(values_col, s):
            return jnp.sum(
                jnp.where(rank_col == s.astype(F32), values_col, 0.0), axis=0, keepdims=True
            ).astype(I32)

        def first(start, residue):
            return start + ((residue - start) & 7)

        zero = jnp.zeros((1, 128), I32)
        half, odd = t >> 1, t & 1
        mine = zero + (plane * 8 + minor)
        start = before(mine)
        end = before(mine + 1)
        s = first(start, half) + 8 * odd
        slot = at_rank(slot_col, s)
        held = (s < end) & (t < 16)
        out_ref[R_T1 + c:R_T1 + c + 1, :] = jnp.where(held, slot, 0)
        out_ref[R_TV + c:R_TV + c + 1, :] = jnp.where(held, slot, -1)

        plane_start = before(zero + plane * 8)
        my_first = first(plane_start, minor)
        s = my_first + 8 * t
        key_s = at_rank(key_col, s)
        start = before(key_s)
        where_n2 = (key_s & 7) * 2 + ((s - first(start, minor)) >> 3)
        out_ref[R_T2 + c:R_T2 + c + 1, :] = jnp.clip(where_n2, 0, 15)

        s = 8 * t + minor
        plane_s = at_rank(key_col, s) >> 3
        place = plane_s * 4 + ((s - first(before(plane_s * 8), minor)) >> 3)
        out_ref[R_T3 + c:R_T3 + c + 1, :] = jnp.clip(place, 0, 31)

        s = 8 * (t & 15) + (t >> 4)
        out_ref[R_O1 + c:R_O1 + c + 1, :] = at_rank(index_col, s)

        s = first(before((t >> 2) * 8), minor) + 8 * (t & 3)
        out_ref[R_O2 + c:R_O2 + c + 1, :] = jnp.clip((s - minor) >> 3, 0, 15)

        s = first(before(zero + plane * 8 + half), minor) + 8 * odd
        out_ref[R_O3 + c:R_O3 + c + 1, :] = jnp.clip((s - my_first) >> 3, 0, 3)

        if c == 0:
            good = good & (before(t + 1) - before(t) <= 16)
        good = good & (before(t * 8 + 8) - before(t * 8) <= 32)
    worst = jnp.min(jnp.where(good, 1.0, 0.0), axis=1, keepdims=True)
    out_ref[R_OK:R_OK + 1, :] = jnp.broadcast_to(worst, (1, 128)).astype(I32)


FAR = (4, 3, 5, 2, 6, 1, 7)


def exchange_kernel(
    pivots_ref, order_ref, linv_ref, uinv_ref, mat_hbm,
    new_out, old_out, opan_out, low_out, linv_out, uinv_out, tab_out, flag_out,
    mat, tabv, tab, pan, mat_sem, tab_sem,
    n1s, n1r, n2s, n2r, o1s, o1r, o2s, o2r, o3s,
    n1_ss, n1_rs, n2_ss, n2_rs, n3_ss, n3_rs, o1_ss, o1_rs, o2_ss, o2_rs, o3_ss, o3_rs,
    p1_ss, p1_rs, p2_ss, p2_rs,
):
    rank = lax.axis_index("row")
    col = lax.axis_index("col")
    z, y = rank // 8, rank % 8
    coords = ((z, y), (y, z))

    def row_of(c, plane, minor):
        return plane * 8 + minor if c == 0 else minor * 8 + plane

    def minor_peer(c, step):
        plane, minor = coords[c]
        other = (minor + step) % 8
        return other, (row_of(c, plane, other), col)

    def plane_peer(c, step):
        plane, minor = coords[c]
        other = (plane + step) % 8
        return other, (row_of(c, other, minor), col)

    def col_peer(step):
        return (rank, (col + step) % 8)

    def copy(src, dst, ssem, rsem, dev):
        return pltpu.make_async_remote_copy(
            src_ref=src, dst_ref=dst, send_sem=ssem, recv_sem=rsem,
            device_id=dev, device_id_type=MESH,
        )

    new2d = new_out.reshape(2 * 8 * 128, 128)

    barrier = pltpu.get_barrier_semaphore()
    for step in range(1, 8):
        for dev in (minor_peer(0, step)[1], minor_peer(1, step)[1], col_peer(step)):
            pl.semaphore_signal(barrier, inc=1, device_id=dev, device_id_type=MESH)

    fetch = pltpu.make_async_copy(mat_hbm, mat, mat_sem)
    fetch.start()
    fill_tables(z, y, pivots_ref, tabv)
    to_scalar = pltpu.make_async_copy(tabv, tab, tab_sem)
    to_scalar.start()
    to_scalar.wait()
    fetch.wait()

    def entry(table, k, top):
        return jnp.clip(tab[table, k], 0, top)

    def mat_tile(row, c):
        return mat[row * 2 + c]

    for c in range(2):
        for k in range(16):
            n1s[c, k] = mat_tile(entry(R_T1 + c, k, 255), c)

    pl.semaphore_wait(barrier, 21)

    n1 = []
    for step in FAR:
        for c in range(2):
            other, dev = minor_peer(c, step)
            minor = coords[c][1]
            d = copy(n1s.at[c, pl.ds(2 * other, 2)], n1r.at[c, pl.ds(2 * minor, 2)],
                     n1_ss.at[c, step], n1_rs.at[c, step], dev)
            d.start()
            n1.append(d)

    o1 = []
    for step in FAR:
        for c in range(2):
            dev = (step if c == 0 else step * 8, col)
            o1.append(copy(o1s.at[c, pl.ds(16 * step, 16)], o1r.at[c],
                           o1_ss.at[c, step], o1_rs.at[c], dev))

    @pl.when(rank == 0)
    def _():
        for n, step in enumerate((*FAR, 0)):
            def body(k, carry):
                for c in range(2):
                    o1s[c, 16 * step + k] = mat_tile(entry(R_O1 + c, 16 * step + k, 127), c)
                return carry
            lax.fori_loop(0, 16, body, 0, unroll=4)
            if step:
                o1[2 * n].start()
                o1[2 * n + 1].start()
        for c in range(2):
            o1r[c] = o1s[c, pl.ds(0, 16)]

    p1 = []
    for step in range(1, 8):
        p1.append(copy(pan, pan, p1_ss.at[step], p1_rs, (rank, step)))

    @pl.when(col == 0)
    def _():
        pan[...] = mat.reshape(4096, 128)[pl.ds(0, 256, stride=16), :]
        for d in p1:
            d.start()

    for c in range(2):
        minor = coords[c][1]
        n1r[c, pl.ds(2 * minor, 2)] = n1s[c, pl.ds(2 * minor, 2)]

    sub = lax.broadcasted_iota(I32, (128, 128), 0)
    order_hot = (sub == order_ref[...]).astype(BF16)
    uinv = uinv_ref[...].astype(F32)
    u_high = jnp.floor(uinv * (1.0 / 256.0))
    u_low = uinv - 256.0 * u_high
    uperm = 256.0 * jnp.dot(order_hot, u_high.astype(BF16), preferred_element_type=F32) + jnp.dot(
        order_hot, u_low.astype(BF16), preferred_element_type=F32
    )
    uinv_out[...] = plain_digits(centred(uperm))
    linv = linv_ref[...].astype(F32)
    for c in range(2):
        hot = (sub == tabv[R_O1 + c:R_O1 + c + 1, :]).astype(BF16)
        linv_out[c] = scaled_digits(one_hot_columns(linv, hot))

    for d in n1:
        d.wait_recv()

    n2 = []
    for c in range(2):
        plane = coords[c][0]
        for j in range(4):
            row = n1r[c, entry(R_T2 + c, j, 15)]
            n2s[c, j] = row
            n2r[c, plane * 4 + j] = row
    for step in FAR:
        for c in range(2):
            plane = coords[c][0]
            other, dev = plane_peer(c, step)
            d = copy(n2s.at[c], n2r.at[c, pl.ds(4 * plane, 4)],
                     n2_ss.at[c, step], n2_rs.at[c, step], dev)
            d.start()
            n2.append(d)

    o2 = [[], []]
    for c in range(2):
        plane, minor = coords[c]
        for step in FAR:
            dev = (row_of(c, step, minor), col)
            o2[c].append(copy(o2s.at[c, pl.ds(4 * step, 4)], o2r.at[c],
                              o2_ss.at[c, step], o2_rs.at[c], dev))

    def do_o2():
        for c in range(2):
            plane, minor = coords[c]

            @pl.when((plane == 0) & (minor != 0))
            def _():
                copy(o1s.at[c, pl.ds(0, 16)], o1r.at[c], o1_ss.at[c, 0], o1_rs.at[c],
                     (0, col)).wait_recv()

            @pl.when(plane == 0)
            def _():
                def body(v, carry):
                    o2s[c, v] = o1r[c, entry(R_O2 + c, v, 15)]
                    return carry
                lax.fori_loop(0, 32, body, 0)
                for d in o2[c]:
                    d.start()
                o2r[c] = o2s[c, pl.ds(0, 4)]

    for d in n2:
        d.wait_recv()

    for c in range(2):
        minor = coords[c][1]
        for k in range(16):
            row = n2r[c, entry(R_T3 + c, k, 31)]
            new2d[pl.ds(c * 1024 + minor * 16 + k, 8, stride=128), :] = row

    sends = []

    def hop_copies(h):
        found = []
        for q in range(2):
            for c in range(2):
                minor = coords[c][1]
                for way in range(2):
                    if h == 4 and q != way:
                        continue
                    sign = 1 if way == 0 else -1
                    block = (minor - sign * (h - 1)) % 8
                    part = new_out.at[c, pl.ds(4 * q, 4), pl.ds(pl.multiple_of(16 * block, 16), 16), :]
                    found.append(copy(part, part, n3_ss.at[c, h, way, q], n3_rs.at[c, h, way, q],
                                      minor_peer(c, sign)[1]))
        return found

    hops = {h: hop_copies(h) for h in range(1, 5)}

    def key(h):
        return [(q, c, way) for q in range(2) for c in range(2) for way in range(2)
                if not (h == 4 and q != way)]

    for d in hops[1]:
        d.start()
    do_o2()

    @pl.when(col != 0)
    def _():
        p1[0].wait_recv()

    low_out[...] = centred(product(scaled_digits(pan[...]), uinv_out[...]))
    for h in range(2, 5):
        before = dict(zip(key(h - 1), hops[h - 1]))
        now = dict(zip(key(h), hops[h]))
        for k in key(h - 1):
            before[k].wait_recv()
            if k in now:
                now[k].start()
        if h == 2:
            o3 = []
            for c in range(2):
                @pl.when(coords[c][0] != 0)
                def _():
                    o2[c][0].wait_recv()

            for c in range(2):
                minor = coords[c][1]
                for k in range(16):
                    o3s[c, k] = o2r[c, entry(R_O3 + c, k, 3)]
                old_out[c, pl.ds(2 * minor, 2)] = o3s[c, pl.ds(2 * minor, 2)]
                for step in FAR:
                    other, dev = minor_peer(c, step)
                    d = copy(o3s.at[c, pl.ds(2 * other, 2)], old_out.at[c, pl.ds(2 * minor, 2)],
                             o3_ss.at[c, step], o3_rs.at[c, step], dev)
                    d.start()
                    o3.append(d)
    for d in o3:
        d.wait_recv()
    p2 = []
    for step in range(1, 8):
        p2.append(copy(opan_out, opan_out, p2_ss.at[step], p2_rs, (rank, step)))

    @pl.when(col == 0)
    def _():
        for k in range(16):
            opan_out[k:k + 1, :] = old_out[0, k, 0:1, :]
        for d in p2:
            d.start()

    for d in hops[4]:
        d.wait_recv()

    @pl.when(col != 0)
    def _():
        p2[0].wait_recv()

    for c in range(2):
        for k in range(16):
            tab_out[c, k] = tab[R_TV + c, k]
    flag_out[0] = tab[R_OK, 0]

    for d in n1 + n2 + o3 + [d for h in hops for d in hops[h]]:
        d.wait_send()

    @pl.when(rank == 0)
    def _():
        for d in o1:
            d.wait_send()

    for c in range(2):
        @pl.when(coords[c][0] == 0)
        def _():
            for d in o2[c]:
                d.wait_send()

    @pl.when(col == 0)
    def _():
        for d in p1 + p2:
            d.wait_send()


def exchange(pivot_rows, column_order, linv, uinv, mat):
    vmem = pl.BlockSpec(memory_space=pltpu.VMEM)
    smem = pl.BlockSpec(memory_space=pltpu.SMEM)
    dma = pltpu.SemaphoreType.DMA
    tile = lambda *lead: pltpu.VMEM((*lead, 8, 128), F32)
    return pl.pallas_call(
        exchange_kernel,
        name="exchange",
        out_shape=(
            jax.ShapeDtypeStruct((2, 8, 128, 128), F32),
            jax.ShapeDtypeStruct((2, 16, 8, 128), F32),
            jax.ShapeDtypeStruct((16, 128), F32),
            jax.ShapeDtypeStruct((256, 128), F32),
            jax.ShapeDtypeStruct((2, 256, 256), BF16),
            jax.ShapeDtypeStruct((256, 128), BF16),
            jax.ShapeDtypeStruct((2, 16), I32),
            jax.ShapeDtypeStruct((1,), I32),
        ),
        in_specs=[vmem] * 4 + [pl.BlockSpec(memory_space=pl.ANY)],
        out_specs=(vmem,) * 6 + (smem, smem),
        scratch_shapes=[
            tile(512), pltpu.VMEM((16, 128), I32), pltpu.SMEM((16, 128), I32),
            pltpu.VMEM((256, 128), F32), dma, dma,
            tile(2, 16), tile(2, 16), tile(2, 4), tile(2, 32), tile(2, 128), tile(2, 16),
            tile(2, 32), tile(2, 4), tile(2, 16),
            dma((2, 8)), dma((2, 8)), dma((2, 8)), dma((2, 8)),
            dma((2, 5, 2, 2)), dma((2, 5, 2, 2)),
            dma((2, 8)), dma((2,)), dma((2, 8)), dma((2,)), dma((2, 8)), dma((2, 8)),
            dma((8,)), dma, dma((8,)), dma,
        ],
        compiler_params=pltpu.CompilerParams(
            collective_id=0, has_side_effects=True, vmem_limit_bytes=24 << 20
        ),
    )(pivot_rows.reshape(1, 128), column_order.reshape(1, 128), linv, uinv, mat)


def update_kernel(
    tab, new_ref, old_ref, opan_ref, low_ref, linv_d, uinv_d, order_ref, mat_hbm,
    out_hbm, mat, low, low_d, up_d, out, sem, out_sem,
):
    rank, col = lax.axis_index("row"), lax.axis_index("col")
    fetch = pltpu.make_async_copy(mat_hbm, mat, sem)
    fetch.start()
    sub = lax.broadcasted_iota(I32, (128, 128), 0)
    eye = sub == lax.broadcasted_iota(I32, (128, 128), 1)
    mat2d = mat.reshape(4096, 128)
    out2d = out.reshape(4096, 128)

    low[...] = low_ref[...]
    old_low = centred(product(scaled_digits(opan_ref[...]), uinv_d[...]))
    for k in range(16):
        slot = tab[0, k]

        @pl.when(slot >= 0)
        def _():
            low[pl.ds(slot, 1), :] = old_low[k:k + 1, :]
    lower = low[...]
    top = jnp.where(rank == 0, jnp.where(eye, -1.0, 0.0), lower[:128])
    low_d[0] = scaled_digits(top)
    low_d[1] = scaled_digits(lower[128:])

    first_upper = None
    for pair in range(8):
        c, e = pair // 4, (pair % 4) * 2
        x = jnp.concatenate([new_ref[c, e], new_ref[c, e + 1]], axis=1)
        upper = centred(product(linv_d[c], plain_digits(x)))
        if pair == 0:
            first_upper = upper[:, :128]
        up_d[pair] = plain_digits(upper)

    fetch.wait()
    for k in range(16):
        for c in range(2):
            slot = tab[c, k]

            @pl.when(slot >= 0)
            def _():
                mat[slot, c] = old_ref[c, k]

    @pl.when(rank == 0)
    def _():
        mat[0:128] = jnp.zeros((128, 2, 8, 128), F32)

    sent = []
    for half in range(2):
        for pair in range(8):
            c = pair // 4
            change = product(low_d[half], up_d[pair])
            for side in range(2):
                rows = pl.ds(2048 * half + 2 * pair + side, 128, stride=16)
                value = mat2d[rows, :] - change[:, 128 * side:128 * side + 128]
                out2d[rows, :] = value - PF * jnp.floor((value + 0.5) * INV)
            if pair == 0:
                @pl.when(col == 0)
                def _():
                    part = low[128 * half:128 * half + 128, :]
                    out2d[pl.ds(2048 * half, 128, stride=16), :] = jnp.where(
                        part < 0.0, part + PF, part
                    )

                if half == 0:
                    @pl.when((col == 0) & (rank == 0))
                    def _():
                        order_hot = (sub == order_ref[...]).astype(BF16)
                        upper = jnp.where(first_upper < 0.0, first_upper + PF, first_upper)
                        out2d[pl.ds(0, 128, stride=16), :] = one_hot_columns(upper, order_hot)
            if pair % 4 == 3:
                where = (pl.ds(128 * half, 128), c)
                d = pltpu.make_async_copy(out.at[where], out_hbm.at[where], out_sem.at[half, c])
                d.start()
                sent.append(d)
    for d in sent:
        d.wait()


def update(tab, new, old, old_panel, low, linv_d, uinv_d, column_order, mat):
    vmem = pl.BlockSpec(memory_space=pltpu.VMEM)
    whole = pltpu.VMEM((256, 2, 8, 128), F32)
    return pl.pallas_call(
        update_kernel,
        name="update",
        out_shape=jax.ShapeDtypeStruct((256, 2, 8, 128), F32),
        in_specs=[pl.BlockSpec(memory_space=pltpu.SMEM)] + [vmem] * 7
        + [pl.BlockSpec(memory_space=pl.ANY)],
        out_specs=pl.BlockSpec(memory_space=pl.ANY),
        scratch_shapes=[
            whole,
            pltpu.VMEM((256, 128), F32),
            pltpu.VMEM((2, 256, 256), BF16),
            pltpu.VMEM((8, 256, 256), BF16),
            whole,
            pltpu.SemaphoreType.DMA,
            pltpu.SemaphoreType.DMA((2, 2)),
        ],
        compiler_params=pltpu.CompilerParams(vmem_limit_bytes=24 << 20),
    )(tab, new, old, old_panel, low, linv_d, uinv_d, column_order.reshape(1, 128), mat)


def on_device(matrix, pivot_rows, column_order, lower_inverse, upper_inverse):
    new, old, old_panel, low, linv_d, uinv_d, tab, flag = exchange(
        pivot_rows, column_order, lower_inverse, upper_inverse, matrix.reshape(512, 8, 128)
    )
    return lax.cond(
        flag[0] > 0,
        lambda: update(tab, new, old, old_panel, low, linv_d, uinv_d, column_order,
                       matrix.reshape(256, 2, 8, 128)).reshape(matrix.shape),
        lambda: general_path(matrix, pivot_rows, column_order, lower_inverse, upper_inverse),
    )


def solution(mesh):
    return jax.shard_map(
        on_device,
        mesh=mesh,
        in_specs=(P(None, "row", None, "col"), P(), P(), P(), P()),
        out_specs=P(None, "row", None, "col"),
        check_vma=False,
    )
```

```python
import jax
import jax.numpy as jnp
from jax import lax
from jax.experimental import pallas as pl
from jax.experimental.pallas import tpu as pltpu
from jax.sharding import PartitionSpec as P

PF = 32749.0
INV = 1.0 / 32749.0
MESH = pl.DeviceIdType.MESH
F32 = jnp.float32
BF16 = jnp.bfloat16
I32 = jnp.int32


def sum_over(array, axis):
    count = lax.axis_size(axis)
    step = 1
    while step < count:
        array = array + lax.ppermute(array, axis, [(i, i ^ step) for i in range(count)])
        step *= 2
    return array


def general_path(matrix, pivot_rows, column_order, lower_inverse, upper_inverse):
    row_cycles = matrix.shape[0]
    panel_width = matrix.shape[1]
    col_cycles = matrix.shape[2]
    local_rows = row_cycles * panel_width
    local_cols = col_cycles * panel_width
    row_count = lax.axis_size("row")
    row_rank = lax.axis_index("row")
    col_rank = lax.axis_index("col")
    flat = matrix.reshape(local_rows, local_cols)
    stride = row_count * panel_width
    owner = pivot_rows % stride // panel_width
    local_slot = pivot_rows // stride * panel_width + pivot_rows % panel_width
    owned = owner == row_rank
    picked = jnp.where(owned[:, None], flat[jnp.where(owned, local_slot, 0)], 0.0)
    top_rows = jnp.where(row_rank == 0, flat[:panel_width], 0.0)
    new_top, old_top = sum_over(picked, "row"), sum_over(top_rows, "row")
    upper_all = modular_product(lower_inverse.astype(F32), new_top)
    targets = jnp.where(owned, local_slot, local_rows)
    swapped = flat.at[targets].set(old_top, mode="drop")
    panel = swapped[:, :panel_width][:, column_order]
    panel_all = sum_over(jnp.where(col_rank == 0, panel, 0.0), "col")
    lower_all = modular_product(panel_all, upper_inverse.astype(F32))
    permuted = upper_all.at[:, :panel_width].set(upper_all[:, column_order])
    upper_use = jnp.where(col_rank == 0, permuted, upper_all)
    result = swapped - modular_product(lower_all, upper_use)
    result = jnp.where(result < 0.0, result + PF, result)
    result = result.at[:, :panel_width].set(
        jnp.where(col_rank == 0, lower_all, result[:, :panel_width])
    )
    result = result.at[:panel_width].set(jnp.where(row_rank == 0, upper_use, result[:panel_width]))
    return result.reshape(row_cycles, panel_width, col_cycles, panel_width)


def centred(x):
    return x - PF * jnp.floor(x * INV + 0.5)


def scaled_digits(a):
    a = centred(a)
    b = centred(a * 256.0)
    both = jnp.concatenate([b, a], axis=1)
    high = jnp.floor(both * (1.0 / 128.0) + 0.5)
    return jnp.concatenate([high, both - 128.0 * high], axis=0).astype(BF16)


def plain_digits(x):
    high = jnp.floor(x * (1.0 / 256.0) + 0.5)
    return jnp.concatenate([high.astype(BF16), (x - 256.0 * high).astype(BF16)], axis=0)


def product(left, right):
    both = jnp.dot(left, right, preferred_element_type=F32)
    rows = both.shape[0] // 2
    return centred(both[:rows]) * 128.0 + both[rows:]


def modular_product(left, right):
    rest = centred(product(scaled_digits(left), plain_digits(right)))
    return jnp.where(rest < 0.0, rest + PF, rest)


def one_hot_columns(values, hot):
    high = jnp.floor(values * (1.0 / 256.0))
    low = values - 256.0 * high
    return 256.0 * jnp.dot(high.astype(BF16), hot, preferred_element_type=F32) + jnp.dot(
        low.astype(BF16), hot, preferred_element_type=F32
    )


R_T1, R_T2, R_T3, R_O1, R_O2, R_O3, R_TV, R_OK = 0, 2, 4, 6, 8, 10, 12, 14


def fill_tables(my_z, my_y, pivots_ref, out_ref):
    sub = lax.broadcasted_iota(I32, (128, 128), 0)
    lane = lax.broadcasted_iota(I32, (128, 128), 1)
    eye = sub == lane
    t = lax.broadcasted_iota(I32, (1, 128), 1)
    pivots = pivots_ref[...]

    def column(row):
        return jnp.sum(jnp.where(eye, row.astype(F32), 0.0), axis=1, keepdims=True)

    owner = (pivots & 8191) >> 7
    slot_col = column(((pivots >> 13) << 7) | (pivots & 127))
    index_col = lax.broadcasted_iota(I32, (128, 1), 0).astype(F32)
    good = jnp.ones((1, 128), jnp.bool_)
    out_ref[...] = jnp.zeros_like(out_ref)
    for c in range(2):
        if c == 0:
            key, plane, minor = owner, my_z, my_y
        else:
            key, plane, minor = ((owner & 7) << 3) | (owner >> 3), my_y, my_z
        key_col = column(key)
        full_row = (key * 128 + t).astype(F32)
        full_col = key_col * 128.0 + index_col
        rank_col = jnp.sum(jnp.where(full_row < full_col, 1.0, 0.0), axis=1, keepdims=True)

        def before(x):
            return jnp.sum(
                jnp.where(key_col < x.astype(F32), 1.0, 0.0), axis=0, keepdims=True
            ).astype(I32)

        def at_rank(values_col, s):
            return jnp.sum(
                jnp.where(rank_col == s.astype(F32), values_col, 0.0), axis=0, keepdims=True
            ).astype(I32)

        def first(start, residue):
            return start + ((residue - start) & 7)

        zero = jnp.zeros((1, 128), I32)
        half, odd = t >> 1, t & 1
        mine = zero + (plane * 8 + minor)
        start = before(mine)
        end = before(mine + 1)
        s = first(start, half) + 8 * odd
        slot = at_rank(slot_col, s)
        held = (s < end) & (t < 16)
        out_ref[R_T1 + c:R_T1 + c + 1, :] = jnp.where(held, slot, 0)
        out_ref[R_TV + c:R_TV + c + 1, :] = jnp.where(held, slot, -1)

        plane_start = before(zero + plane * 8)
        my_first = first(plane_start, minor)
        s = my_first + 8 * t
        key_s = at_rank(key_col, s)
        start = before(key_s)
        where_n2 = (key_s & 7) * 2 + ((s - first(start, minor)) >> 3)
        out_ref[R_T2 + c:R_T2 + c + 1, :] = jnp.clip(where_n2, 0, 15)

        s = 8 * t + minor
        plane_s = at_rank(key_col, s) >> 3
        place = plane_s * 4 + ((s - first(before(plane_s * 8), minor)) >> 3)
        out_ref[R_T3 + c:R_T3 + c + 1, :] = jnp.clip(place, 0, 31)

        s = 8 * (t & 15) + (t >> 4)
        out_ref[R_O1 + c:R_O1 + c + 1, :] = at_rank(index_col, s)

        s = first(before((t >> 2) * 8), minor) + 8 * (t & 3)
        out_ref[R_O2 + c:R_O2 + c + 1, :] = jnp.clip((s - minor) >> 3, 0, 15)

        s = first(before(zero + plane * 8 + half), minor) + 8 * odd
        out_ref[R_O3 + c:R_O3 + c + 1, :] = jnp.clip((s - my_first) >> 3, 0, 3)

        if c == 0:
            good = good & (before(t + 1) - before(t) <= 16)
        good = good & (before(t * 8 + 8) - before(t * 8) <= 32)
    worst = jnp.min(jnp.where(good, 1.0, 0.0), axis=1, keepdims=True)
    out_ref[R_OK:R_OK + 1, :] = jnp.broadcast_to(worst, (1, 128)).astype(I32)


FAR = (4, 3, 5, 2, 6, 1, 7)


def exchange_kernel(
    pivots_ref, order_ref, linv_ref, uinv_ref, mat_hbm,
    new_out, old_out, opan_out, low_out, linv_out, uinv_out, tab_out, flag_out,
    mat, tabv, tab, pan, mat_sem, tab_sem,
    n1s, n1r, n2s, n2r, o1s, o1r, o2s, o2r, o3s,
    n1_ss, n1_rs, n2_ss, n2_rs, n3_ss, n3_rs, o1_ss, o1_rs, o2_ss, o2_rs, o3_ss, o3_rs,
    p1_ss, p1_rs, p2_ss, p2_rs,
):
    rank = lax.axis_index("row")
    col = lax.axis_index("col")
    z, y = rank // 8, rank % 8
    coords = ((z, y), (y, z))

    def row_of(c, plane, minor):
        return plane * 8 + minor if c == 0 else minor * 8 + plane

    def minor_peer(c, step):
        plane, minor = coords[c]
        other = (minor + step) % 8
        return other, (row_of(c, plane, other), col)

    def plane_peer(c, step):
        plane, minor = coords[c]
        other = (plane + step) % 8
        return other, (row_of(c, other, minor), col)

    def col_peer(step):
        return (rank, (col + step) % 8)

    def copy(src, dst, ssem, rsem, dev):
        return pltpu.make_async_remote_copy(
            src_ref=src, dst_ref=dst, send_sem=ssem, recv_sem=rsem,
            device_id=dev, device_id_type=MESH,
        )

    new2d = new_out.reshape(2 * 8 * 128, 128)

    barrier = pltpu.get_barrier_semaphore()
    for step in range(1, 8):
        for dev in (minor_peer(0, step)[1], minor_peer(1, step)[1], col_peer(step)):
            pl.semaphore_signal(barrier, inc=1, device_id=dev, device_id_type=MESH)

    fetch = pltpu.make_async_copy(mat_hbm, mat, mat_sem)
    fetch.start()
    fill_tables(z, y, pivots_ref, tabv)
    to_scalar = pltpu.make_async_copy(tabv, tab, tab_sem)
    to_scalar.start()
    to_scalar.wait()
    fetch.wait()

    def entry(table, k, top):
        return jnp.clip(tab[table, k], 0, top)

    def mat_tile(row, c):
        return mat[row * 2 + c]

    for c in range(2):
        for k in range(16):
            n1s[c, k] = mat_tile(entry(R_T1 + c, k, 255), c)

    pl.semaphore_wait(barrier, 21)

    n1 = []
    for step in FAR:
        for c in range(2):
            other, dev = minor_peer(c, step)
            minor = coords[c][1]
            d = copy(n1s.at[c, pl.ds(2 * other, 2)], n1r.at[c, pl.ds(2 * minor, 2)],
                     n1_ss.at[c, step], n1_rs.at[c, step], dev)
            d.start()
            n1.append(d)

    o1 = []
    for step in FAR:
        for c in range(2):
            dev = (step if c == 0 else step * 8, col)
            o1.append(copy(o1s.at[c, pl.ds(16 * step, 16)], o1r.at[c],
                           o1_ss.at[c, step], o1_rs.at[c], dev))

    @pl.when(rank == 0)
    def _():
        for n, step in enumerate((*FAR, 0)):
            def body(k, carry):
                for c in range(2):
                    o1s[c, 16 * step + k] = mat_tile(entry(R_O1 + c, 16 * step + k, 127), c)
                return carry
            lax.fori_loop(0, 16, body, 0, unroll=4)
            if step:
                o1[2 * n].start()
                o1[2 * n + 1].start()
        for c in range(2):
            o1r[c] = o1s[c, pl.ds(0, 16)]

    p1 = []
    for step in range(1, 8):
        p1.append(copy(pan, pan, p1_ss.at[step], p1_rs, (rank, step)))

    @pl.when(col == 0)
    def _():
        pan[...] = mat.reshape(4096, 128)[pl.ds(0, 256, stride=16), :]
        for d in p1:
            d.start()

    for c in range(2):
        minor = coords[c][1]
        n1r[c, pl.ds(2 * minor, 2)] = n1s[c, pl.ds(2 * minor, 2)]

    sub = lax.broadcasted_iota(I32, (128, 128), 0)
    order_hot = (sub == order_ref[...]).astype(BF16)
    uinv = uinv_ref[...].astype(F32)
    u_high = jnp.floor(uinv * (1.0 / 256.0))
    u_low = uinv - 256.0 * u_high
    uperm = 256.0 * jnp.dot(order_hot, u_high.astype(BF16), preferred_element_type=F32) + jnp.dot(
        order_hot, u_low.astype(BF16), preferred_element_type=F32
    )
    uinv_out[...] = plain_digits(centred(uperm))
    linv = linv_ref[...].astype(F32)
    for c in range(2):
        hot = (sub == tabv[R_O1 + c:R_O1 + c + 1, :]).astype(BF16)
        linv_out[c] = scaled_digits(one_hot_columns(linv, hot))

    for d in n1:
        d.wait_recv()

    n2 = []
    for c in range(2):
        plane = coords[c][0]
        for j in range(4):
            row = n1r[c, entry(R_T2 + c, j, 15)]
            n2s[c, j] = row
            n2r[c, plane * 4 + j] = row
    for step in FAR:
        for c in range(2):
            plane = coords[c][0]
            other, dev = plane_peer(c, step)
            d = copy(n2s.at[c], n2r.at[c, pl.ds(4 * plane, 4)],
                     n2_ss.at[c, step], n2_rs.at[c, step], dev)
            d.start()
            n2.append(d)

    o2 = [[], []]
    for c in range(2):
        plane, minor = coords[c]
        for step in FAR:
            dev = (row_of(c, step, minor), col)
            o2[c].append(copy(o2s.at[c, pl.ds(4 * step, 4)], o2r.at[c],
                              o2_ss.at[c, step], o2_rs.at[c], dev))

    for c in range(2):
        plane, minor = coords[c]

        @pl.when((plane == 0) & (minor != 0))
        def _():
            copy(o1s.at[c, pl.ds(0, 16)], o1r.at[c], o1_ss.at[c, 0], o1_rs.at[c],
                 (0, col)).wait_recv()

        @pl.when(plane == 0)
        def _():
            def body(v, carry):
                o2s[c, v] = o1r[c, entry(R_O2 + c, v, 15)]
                return carry
            lax.fori_loop(0, 32, body, 0)
            for d in o2[c]:
                d.start()
            o2r[c] = o2s[c, pl.ds(0, 4)]

    for d in n2:
        d.wait_recv()

    for c in range(2):
        minor = coords[c][1]
        for k in range(16):
            row = n2r[c, entry(R_T3 + c, k, 31)]
            new2d[pl.ds(c * 1024 + minor * 16 + k, 8, stride=128), :] = row

    def part(c, block, e, count):
        rows = pl.ds(pl.multiple_of(16 * block, 16), 16)
        return new_out.at[c, pl.ds(e, count), rows, :]

    def n3_copy(c, kind, way, q, block, e, count, offset):
        piece = part(c, block % 8, e, count)
        return copy(piece, piece, n3_ss.at[c, kind, way, q], n3_rs.at[c, kind, way, q],
                    minor_peer(c, offset)[1])

    both = [(c, way) for c in range(2) for way in range(2)]
    two, one, three, four = {}, {}, {}, {}
    for c, way in both:
        minor = coords[c][1]
        sign = 1 - 2 * way
        one[c, way] = n3_copy(c, 1, way, 0, minor, 0, 8, sign)
        for n in range(2):
            q = n if way == 0 else 1 - n
            two[c, way, n] = n3_copy(c, 0, way, n, minor, 4 * q, 4, 2 * sign)
            three[c, way, n] = n3_copy(c, 2, way, n, minor - 2 * sign, 4 * q, 4, sign)
        four[c, way] = n3_copy(c, 3, way, 0, minor - 2 * sign, 4 * way, 4, 2 * sign)
    for n in range(2):
        for c, way in both:
            two[c, way, n].start()
    for c, way in both:
        one[c, way].start()

    for c in range(2):
        @pl.when(coords[c][0] != 0)
        def _():
            o2[c][0].wait_recv()

    o3 = []
    for c in range(2):
        minor = coords[c][1]
        for k in range(16):
            o3s[c, k] = o2r[c, entry(R_O3 + c, k, 3)]
        old_out[c, pl.ds(2 * minor, 2)] = o3s[c, pl.ds(2 * minor, 2)]
        for step in FAR:
            other, dev = minor_peer(c, step)
            d = copy(o3s.at[c, pl.ds(2 * other, 2)], old_out.at[c, pl.ds(2 * minor, 2)],
                     o3_ss.at[c, step], o3_rs.at[c, step], dev)
            d.start()
            o3.append(d)

    @pl.when(col != 0)
    def _():
        p1[0].wait_recv()

    low_out[...] = centred(product(scaled_digits(pan[...]), uinv_out[...]))

    for n in range(2):
        for c, way in both:
            two[c, way, n].wait_recv()
            if n == 0:
                four[c, way].start()
            three[c, way, n].start()

    for d in o3:
        d.wait_recv()
    p2 = []
    for step in range(1, 8):
        p2.append(copy(opan_out, opan_out, p2_ss.at[step], p2_rs, (rank, step)))

    @pl.when(col == 0)
    def _():
        for k in range(16):
            opan_out[k:k + 1, :] = old_out[0, k, 0:1, :]
        for d in p2:
            d.start()

    for d in [*one.values(), *three.values(), *four.values()]:
        d.wait_recv()

    @pl.when(col != 0)
    def _():
        p2[0].wait_recv()

    for c in range(2):
        for k in range(16):
            tab_out[c, k] = tab[R_TV + c, k]
    flag_out[0] = tab[R_OK, 0]

    for d in [*n1, *n2, *o3, *one.values(), *two.values(), *three.values(), *four.values()]:
        d.wait_send()

    @pl.when(rank == 0)
    def _():
        for d in o1:
            d.wait_send()

    for c in range(2):
        @pl.when(coords[c][0] == 0)
        def _():
            for d in o2[c]:
                d.wait_send()

    @pl.when(col == 0)
    def _():
        for d in p1 + p2:
            d.wait_send()


def exchange(pivot_rows, column_order, linv, uinv, mat):
    vmem = pl.BlockSpec(memory_space=pltpu.VMEM)
    smem = pl.BlockSpec(memory_space=pltpu.SMEM)
    dma = pltpu.SemaphoreType.DMA
    tile = lambda *lead: pltpu.VMEM((*lead, 8, 128), F32)
    return pl.pallas_call(
        exchange_kernel,
        name="exchange",
        out_shape=(
            pltpu.VMEM((2, 8, 128, 128), F32),
            pltpu.VMEM((2, 16, 8, 128), F32),
            pltpu.VMEM((16, 128), F32),
            pltpu.VMEM((256, 128), F32),
            pltpu.VMEM((2, 256, 256), BF16),
            pltpu.VMEM((256, 128), BF16),
            jax.ShapeDtypeStruct((2, 16), I32),
            jax.ShapeDtypeStruct((1,), I32),
        ),
        in_specs=[vmem] * 4 + [pl.BlockSpec(memory_space=pl.ANY)],
        out_specs=(vmem,) * 6 + (smem, smem),
        scratch_shapes=[
            tile(512), pltpu.VMEM((16, 128), I32), pltpu.SMEM((16, 128), I32),
            pltpu.VMEM((256, 128), F32), dma, dma,
            tile(2, 16), tile(2, 16), tile(2, 4), tile(2, 32), tile(2, 128), tile(2, 16),
            tile(2, 32), tile(2, 4), tile(2, 16),
            dma((2, 8)), dma((2, 8)), dma((2, 8)), dma((2, 8)),
            dma((2, 4, 2, 2)), dma((2, 4, 2, 2)),
            dma((2, 8)), dma((2,)), dma((2, 8)), dma((2,)), dma((2, 8)), dma((2, 8)),
            dma((8,)), dma, dma((8,)), dma,
        ],
        compiler_params=pltpu.CompilerParams(
            collective_id=0, has_side_effects=True, vmem_limit_bytes=24 << 20
        ),
    )(pivot_rows.reshape(1, 128), column_order.reshape(1, 128), linv, uinv, mat)


def update_kernel(
    tab, new_ref, old_ref, opan_ref, low_ref, linv_d, uinv_d, order_ref, mat_hbm,
    out_hbm, mat, low, low_d, up_d, out, sem, out_sem,
):
    rank, col = lax.axis_index("row"), lax.axis_index("col")
    fetch = pltpu.make_async_copy(mat_hbm, mat, sem)
    fetch.start()
    sub = lax.broadcasted_iota(I32, (128, 128), 0)
    eye = sub == lax.broadcasted_iota(I32, (128, 128), 1)
    mat2d = mat.reshape(4096, 128)
    out2d = out.reshape(4096, 128)

    low[...] = low_ref[...]
    old_low = centred(product(scaled_digits(opan_ref[...]), uinv_d[...]))
    for k in range(16):
        slot = tab[0, k]

        @pl.when(slot >= 0)
        def _():
            low[pl.ds(slot, 1), :] = old_low[k:k + 1, :]
    lower = low[...]
    top = jnp.where(rank == 0, jnp.where(eye, -1.0, 0.0), lower[:128])
    low_d[0] = scaled_digits(top)
    low_d[1] = scaled_digits(lower[128:])

    first_upper = None
    for pair in range(8):
        c, e = pair // 4, (pair % 4) * 2
        x = jnp.concatenate([new_ref[c, e], new_ref[c, e + 1]], axis=1)
        upper = centred(product(linv_d[c], plain_digits(x)))
        if pair == 0:
            first_upper = upper[:, :128]
        up_d[pair] = plain_digits(upper)

    fetch.wait()
    for k in range(16):
        for c in range(2):
            slot = tab[c, k]

            @pl.when(slot >= 0)
            def _():
                mat[slot, c] = old_ref[c, k]

    @pl.when(rank == 0)
    def _():
        mat[0:128] = jnp.zeros((128, 2, 8, 128), F32)

    sent = []
    for half in range(2):
        for pair in range(8):
            c = pair // 4
            change = product(low_d[half], up_d[pair])
            for side in range(2):
                rows = pl.ds(2048 * half + 2 * pair + side, 128, stride=16)
                value = mat2d[rows, :] - change[:, 128 * side:128 * side + 128]
                out2d[rows, :] = value - PF * jnp.floor((value + 0.5) * INV)
            if pair == 0:
                @pl.when(col == 0)
                def _():
                    part = low[128 * half:128 * half + 128, :]
                    out2d[pl.ds(2048 * half, 128, stride=16), :] = jnp.where(
                        part < 0.0, part + PF, part
                    )

                if half == 0:
                    @pl.when((col == 0) & (rank == 0))
                    def _():
                        order_hot = (sub == order_ref[...]).astype(BF16)
                        upper = jnp.where(first_upper < 0.0, first_upper + PF, first_upper)
                        out2d[pl.ds(0, 128, stride=16), :] = one_hot_columns(upper, order_hot)
            if pair % 4 == 3:
                where = (pl.ds(128 * half, 128), c)
                d = pltpu.make_async_copy(out.at[where], out_hbm.at[where], out_sem.at[half, c])
                d.start()
                sent.append(d)
    for d in sent:
        d.wait()


def update(tab, new, old, old_panel, low, linv_d, uinv_d, column_order, mat):
    vmem = pl.BlockSpec(memory_space=pltpu.VMEM)
    whole = pltpu.VMEM((256, 2, 8, 128), F32)
    return pl.pallas_call(
        update_kernel,
        name="update",
        out_shape=jax.ShapeDtypeStruct((256, 2, 8, 128), F32),
        in_specs=[pl.BlockSpec(memory_space=pltpu.SMEM)] + [vmem] * 7
        + [pl.BlockSpec(memory_space=pl.ANY)],
        out_specs=pl.BlockSpec(memory_space=pl.ANY),
        scratch_shapes=[
            whole,
            pltpu.VMEM((256, 128), F32),
            pltpu.VMEM((2, 256, 256), BF16),
            pltpu.VMEM((8, 256, 256), BF16),
            whole,
            pltpu.SemaphoreType.DMA,
            pltpu.SemaphoreType.DMA((2, 2)),
        ],
        compiler_params=pltpu.CompilerParams(vmem_limit_bytes=24 << 20),
    )(tab, new, old, old_panel, low, linv_d, uinv_d, column_order.reshape(1, 128), mat)


def on_device(matrix, pivot_rows, column_order, lower_inverse, upper_inverse):
    new, old, old_panel, low, linv_d, uinv_d, tab, flag = exchange(
        pivot_rows, column_order, lower_inverse, upper_inverse, matrix.reshape(512, 8, 128)
    )
    return lax.cond(
        flag[0] > 0,
        lambda: update(tab, new, old, old_panel, low, linv_d, uinv_d, column_order,
                       matrix.reshape(256, 2, 8, 128)).reshape(matrix.shape),
        lambda: general_path(matrix, pivot_rows, column_order, lower_inverse, upper_inverse),
    )


def solution(mesh):
    return jax.shard_map(
        on_device,
        mesh=mesh,
        in_specs=(P(None, "row", None, "col"), P(), P(), P(), P()),
        out_specs=P(None, "row", None, "col"),
        check_vma=False,
    )
```

```python
import jax
import jax.numpy as jnp
from jax import lax
from jax.experimental import pallas as pl
from jax.experimental.pallas import tpu as pltpu
from jax.sharding import PartitionSpec as P

PF = 32749.0
INV = 1.0 / 32749.0
MESH = pl.DeviceIdType.MESH
F32 = jnp.float32
BF16 = jnp.bfloat16
I32 = jnp.int32


def sum_over(array, axis):
    count = lax.axis_size(axis)
    step = 1
    while step < count:
        array = array + lax.ppermute(array, axis, [(i, i ^ step) for i in range(count)])
        step *= 2
    return array


def general_path(matrix, pivot_rows, column_order, lower_inverse, upper_inverse):
    row_cycles = matrix.shape[0]
    panel_width = matrix.shape[1]
    col_cycles = matrix.shape[2]
    local_rows = row_cycles * panel_width
    local_cols = col_cycles * panel_width
    row_count = lax.axis_size("row")
    row_rank = lax.axis_index("row")
    col_rank = lax.axis_index("col")
    flat = matrix.reshape(local_rows, local_cols)
    stride = row_count * panel_width
    owner = pivot_rows % stride // panel_width
    local_slot = pivot_rows // stride * panel_width + pivot_rows % panel_width
    owned = owner == row_rank
    picked = jnp.where(owned[:, None], flat[jnp.where(owned, local_slot, 0)], 0.0)
    top_rows = jnp.where(row_rank == 0, flat[:panel_width], 0.0)
    new_top, old_top = sum_over(picked, "row"), sum_over(top_rows, "row")
    upper_all = modular_product(lower_inverse.astype(F32), new_top)
    targets = jnp.where(owned, local_slot, local_rows)
    swapped = flat.at[targets].set(old_top, mode="drop")
    panel = swapped[:, :panel_width][:, column_order]
    panel_all = sum_over(jnp.where(col_rank == 0, panel, 0.0), "col")
    lower_all = modular_product(panel_all, upper_inverse.astype(F32))
    permuted = upper_all.at[:, :panel_width].set(upper_all[:, column_order])
    upper_use = jnp.where(col_rank == 0, permuted, upper_all)
    result = swapped - modular_product(lower_all, upper_use)
    result = jnp.where(result < 0.0, result + PF, result)
    result = result.at[:, :panel_width].set(
        jnp.where(col_rank == 0, lower_all, result[:, :panel_width])
    )
    result = result.at[:panel_width].set(jnp.where(row_rank == 0, upper_use, result[:panel_width]))
    return result.reshape(row_cycles, panel_width, col_cycles, panel_width)


def centred(x):
    return x - PF * jnp.floor(x * INV + 0.5)


def scaled_digits(a):
    a = centred(a)
    b = centred(a * 256.0)
    both = jnp.concatenate([b, a], axis=1)
    high = 64.0 * jnp.floor(both * (1.0 / 64.0) + 0.5)
    return jnp.concatenate([high, both - high], axis=0).astype(BF16)


def plain_digits(x):
    high = jnp.floor(x * (1.0 / 256.0))
    return jnp.concatenate([high.astype(BF16), (x - 256.0 * high).astype(BF16)], axis=0)


def product(left, right):
    both = jnp.dot(left, right, preferred_element_type=F32)
    rows = both.shape[0] // 2
    high = both[:rows]
    return (high - (64.0 * PF) * jnp.floor(high * (INV / 64.0))) + both[rows:]


def modular_product(left, right):
    rest = centred(product(scaled_digits(left), plain_digits(right)))
    return jnp.where(rest < 0.0, rest + PF, rest)


def one_hot_columns(values, hot):
    high = jnp.floor(values * (1.0 / 256.0))
    low = values - 256.0 * high
    return 256.0 * jnp.dot(high.astype(BF16), hot, preferred_element_type=F32) + jnp.dot(
        low.astype(BF16), hot, preferred_element_type=F32
    )


R_T2, R_T3, R_O1, R_O2, R_O3, R_OK = 2, 4, 6, 8, 10, 14


def fill_tables(my_z, my_y, pivots_ref, first_ref, out_ref):
    sub = lax.broadcasted_iota(I32, (128, 128), 0)
    lane = lax.broadcasted_iota(I32, (128, 128), 1)
    eye = sub == lane
    t = lax.broadcasted_iota(I32, (1, 128), 1)
    pivots = pivots_ref[...]

    def column(row):
        return jnp.sum(jnp.where(eye, row.astype(F32), 0.0), axis=1, keepdims=True)

    owner = (pivots & 8191) >> 7
    slot_col = column(((pivots >> 13) << 7) | (pivots & 127))
    index_col = lax.broadcasted_iota(I32, (128, 1), 0).astype(F32)
    zero = jnp.zeros((1, 128), I32)
    half, odd = t >> 1, t & 1

    def first(start, residue):
        return start + ((residue - start) & 7)

    halves = []
    for c in range(2):
        if c == 0:
            key, plane, minor = owner, my_z, my_y
        else:
            key, plane, minor = ((owner & 7) << 3) | (owner >> 3), my_y, my_z
        key_col = column(key)
        full_row = (key * 128 + t).astype(F32)
        full_col = key_col * 128.0 + index_col
        rank_col = jnp.sum(jnp.where(full_row < full_col, 1.0, 0.0), axis=1, keepdims=True)

        def before(x, key_col=key_col):
            return jnp.sum(
                jnp.where(key_col < x.astype(F32), 1.0, 0.0), axis=0, keepdims=True
            ).astype(I32)

        def at_rank(values_col, s, rank_col=rank_col):
            return jnp.sum(
                jnp.where(rank_col == s.astype(F32), values_col, 0.0), axis=0, keepdims=True
            ).astype(I32)

        mine = zero + (plane * 8 + minor)
        start = before(mine)
        end = before(mine + 1)
        s = first(start, half) + 8 * odd
        slot = at_rank(slot_col, s)
        held = (s < end) & (t < 16)
        slot = jnp.where(held, slot, -1)
        first_ref[c:c + 1, :] = slot
        if c == 0:
            slot_first = column(slot)
        else:
            same = slot_first == slot.astype(F32)
            place = jnp.sum(jnp.where(same, index_col, 0.0), axis=0, keepdims=True)
            first_ref[2:3, :] = place.astype(I32)
        halves.append((plane, minor, key_col, before, at_rank))

    def rest():
        good = jnp.ones((1, 128), jnp.bool_)
        out_ref[...] = jnp.zeros_like(out_ref)
        for c in range(2):
            good = fill_rest(c, good)
        worst = jnp.min(jnp.where(good, 1.0, 0.0), axis=1, keepdims=True)
        out_ref[R_OK:R_OK + 1, :] = jnp.broadcast_to(worst, (1, 128)).astype(I32)

    def fill_rest(c, good):
        plane, minor, key_col, before, at_rank = halves[c]
        plane_start = before(zero + plane * 8)
        my_first = first(plane_start, minor)
        s = my_first + 8 * t
        key_s = at_rank(key_col, s)
        start = before(key_s)
        where_n2 = (key_s & 7) * 2 + ((s - first(start, minor)) >> 3)
        out_ref[R_T2 + c:R_T2 + c + 1, :] = jnp.clip(where_n2, 0, 15)

        s = 8 * t + minor
        plane_s = at_rank(key_col, s) >> 3
        place = plane_s * 4 + ((s - first(before(plane_s * 8), minor)) >> 3)
        out_ref[R_T3 + c:R_T3 + c + 1, :] = jnp.clip(place, 0, 31)

        s = 8 * (t & 15) + (t >> 4)
        out_ref[R_O1 + c:R_O1 + c + 1, :] = at_rank(index_col, s)

        s = first(before((t >> 2) * 8), minor) + 8 * (t & 3)
        out_ref[R_O2 + c:R_O2 + c + 1, :] = jnp.clip((s - minor) >> 3, 0, 15)

        s = first(before(zero + plane * 8 + half), minor) + 8 * odd
        out_ref[R_O3 + c:R_O3 + c + 1, :] = jnp.clip((s - my_first) >> 3, 0, 3)

        if c == 0:
            good = good & (before(t + 1) - before(t) <= 16)
        good = good & (before(t * 8 + 8) - before(t * 8) <= 32)
        return good

    return rest


FAR = (4, 3, 5, 2, 6, 1, 7)


def exchange_kernel(
    pivots_ref, order_ref, linv_ref, uinv_ref, mat_hbm,
    new_out, old_out, opan_out, low_out, low_d_out, linv_out, uinv_out, mat_out, tab_out, flag_out,
    mat, firstv, first, tabv, tab, pan, mat_sem, first_sem, tab_sem,
    n1s, n1r, n2s, n2r, o1s, o1r, o2s, o2r, o3s,
    n1_ss, n1_rs, n2_ss, n2_rs, n3_ss, n3_rs, o1_ss, o1_rs, o2_ss, o2_rs, o3_ss, o3_rs,
    p1_ss, p1_rs, p2_ss, p2_rs,
):
    rank = lax.axis_index("row")
    col = lax.axis_index("col")
    z, y = rank // 8, rank % 8
    coords = ((z, y), (y, z))

    def row_of(c, plane, minor):
        return plane * 8 + minor if c == 0 else minor * 8 + plane

    def minor_peer(c, step):
        plane, minor = coords[c]
        other = (minor + step) % 8
        return other, (row_of(c, plane, other), col)

    def plane_peer(c, step):
        plane, minor = coords[c]
        other = (plane + step) % 8
        return other, (row_of(c, other, minor), col)

    def col_peer(step):
        return (rank, (col + step) % 8)

    def copy(src, dst, ssem, rsem, dev):
        return pltpu.make_async_remote_copy(
            src_ref=src, dst_ref=dst, send_sem=ssem, recv_sem=rsem,
            device_id=dev, device_id_type=MESH,
        )

    new2d = new_out.reshape(2 * 8 * 128, 128)

    barrier = pltpu.get_barrier_semaphore()
    for step in range(1, 8):
        for dev in (minor_peer(0, step)[1], minor_peer(1, step)[1], col_peer(step)):
            pl.semaphore_signal(barrier, inc=1, device_id=dev, device_id_type=MESH)

    fetch = pltpu.make_async_copy(mat_hbm, mat, mat_sem)
    fetch.start()
    fill_rest = fill_tables(z, y, pivots_ref, firstv, tabv)
    to_scalar = pltpu.make_async_copy(firstv, first, first_sem)
    to_scalar.start()
    to_scalar.wait()
    fetch.wait()

    def entry(table, k, top):
        return jnp.clip(tab[table, k], 0, top)

    def mat_tile(row, c):
        return mat[row * 2 + c]

    for c in range(2):
        for k in range(16):
            n1s[c, k] = mat_tile(jnp.clip(first[c, k], 0, 255), c)

    pl.semaphore_wait(barrier, 21)

    n1 = []
    for step in FAR:
        for c in range(2):
            other, dev = minor_peer(c, step)
            minor = coords[c][1]
            d = copy(n1s.at[c, pl.ds(2 * other, 2)], n1r.at[c, pl.ds(2 * minor, 2)],
                     n1_ss.at[c, step], n1_rs.at[c, step], dev)
            d.start()
            n1.append(d)

    fill_rest()
    to_scalar = pltpu.make_async_copy(tabv, tab, tab_sem)
    to_scalar.start()
    to_scalar.wait()

    o1 = []
    for step in FAR:
        for c in range(2):
            dev = (step if c == 0 else step * 8, col)
            o1.append(copy(o1s.at[c, pl.ds(16 * step, 16)], o1r.at[c],
                           o1_ss.at[c, step], o1_rs.at[c], dev))

    @pl.when(rank == 0)
    def _():
        for n, step in enumerate((*FAR, 0)):
            def body(k, carry):
                for c in range(2):
                    o1s[c, 16 * step + k] = mat_tile(entry(R_O1 + c, 16 * step + k, 127), c)
                return carry
            lax.fori_loop(0, 16, body, 0, unroll=4)
            if step:
                o1[2 * n].start()
                o1[2 * n + 1].start()
        for c in range(2):
            o1r[c] = o1s[c, pl.ds(0, 16)]

    p1 = []
    for step in range(1, 8):
        p1.append(copy(pan, pan, p1_ss.at[step], p1_rs, (rank, step)))

    @pl.when(col == 0)
    def _():
        pan[...] = mat.reshape(4096, 128)[pl.ds(0, 256, stride=16), :]
        for d in p1:
            d.start()

    for c in range(2):
        minor = coords[c][1]
        n1r[c, pl.ds(2 * minor, 2)] = n1s[c, pl.ds(2 * minor, 2)]

    mat2d = mat.reshape(4096, 128)
    for e in range(16):
        upper_half = mat2d[pl.ds(e, 128, stride=16), :]
        mat_out[e, 0:128, :] = jnp.where(rank == 0, 0.0, upper_half)
        mat_out[e, 128:256, :] = mat2d[pl.ds(2048 + e, 128, stride=16), :]
    sub = lax.broadcasted_iota(I32, (128, 128), 0)
    eye = sub == lax.broadcasted_iota(I32, (128, 128), 1)
    order_hot = (sub == order_ref[...]).astype(BF16)
    uinv = uinv_ref[...].astype(F32)
    u_high = jnp.floor(uinv * (1.0 / 256.0))
    u_low = uinv - 256.0 * u_high
    uperm = 256.0 * jnp.dot(order_hot, u_high.astype(BF16), preferred_element_type=F32) + jnp.dot(
        order_hot, u_low.astype(BF16), preferred_element_type=F32
    )
    uinv_out[...] = plain_digits(centred(uperm))
    linv = linv_ref[...].astype(F32)
    for c in range(2):
        hot = (sub == tabv[R_O1 + c:R_O1 + c + 1, :]).astype(BF16)
        linv_out[c] = scaled_digits(one_hot_columns(linv, hot))

    for d in n1:
        d.wait_recv()

    n2 = []
    for c in range(2):
        plane = coords[c][0]
        for j in range(4):
            row = n1r[c, entry(R_T2 + c, j, 15)]
            n2s[c, j] = row
            n2r[c, plane * 4 + j] = row
    for step in FAR:
        for c in range(2):
            plane = coords[c][0]
            other, dev = plane_peer(c, step)
            d = copy(n2s.at[c], n2r.at[c, pl.ds(4 * plane, 4)],
                     n2_ss.at[c, step], n2_rs.at[c, step], dev)
            d.start()
            n2.append(d)

    o2 = [[], []]
    for c in range(2):
        plane, minor = coords[c]
        for step in FAR:
            dev = (row_of(c, step, minor), col)
            o2[c].append(copy(o2s.at[c, pl.ds(4 * step, 4)], o2r.at[c],
                              o2_ss.at[c, step], o2_rs.at[c], dev))

    for c in range(2):
        plane, minor = coords[c]

        @pl.when((plane == 0) & (minor != 0))
        def _():
            copy(o1s.at[c, pl.ds(0, 16)], o1r.at[c], o1_ss.at[c, 0], o1_rs.at[c],
                 (0, col)).wait_recv()

        @pl.when(plane == 0)
        def _():
            def body(v, carry):
                o2s[c, v] = o1r[c, entry(R_O2 + c, v, 15)]
                return carry
            lax.fori_loop(0, 32, body, 0)
            for d in o2[c]:
                d.start()
            o2r[c] = o2s[c, pl.ds(0, 4)]

    for d in n2:
        d.wait_recv()

    for c in range(2):
        minor = coords[c][1]
        for k in range(16):
            row = n2r[c, entry(R_T3 + c, k, 31)]
            new2d[pl.ds(c * 1024 + minor * 16 + k, 8, stride=128), :] = row

    def part(c, block, e, count):
        rows = pl.ds(pl.multiple_of(16 * block, 16), 16)
        return new_out.at[c, pl.ds(e, count), rows, :]

    def n3_copy(c, kind, way, q, block, e, count, offset):
        piece = part(c, block % 8, e, count)
        return copy(piece, piece, n3_ss.at[c, kind, way, q], n3_rs.at[c, kind, way, q],
                    minor_peer(c, offset)[1])

    both = [(c, way) for c in range(2) for way in range(2)]
    two, one, three, four = {}, {}, {}, {}
    for c, way in both:
        minor = coords[c][1]
        sign = 1 - 2 * way
        one[c, way] = n3_copy(c, 1, way, 0, minor, 0, 8, sign)
        for n in range(2):
            q = n if way == 0 else 1 - n
            two[c, way, n] = n3_copy(c, 0, way, n, minor, 4 * q, 4, 2 * sign)
            three[c, way, n] = n3_copy(c, 2, way, n, minor - 2 * sign, 4 * q, 4, sign)
        four[c, way] = n3_copy(c, 3, way, 0, minor - 2 * sign, 4 * way, 4, 2 * sign)
    for n in range(2):
        for c, way in both:
            two[c, way, n].start()
    for c, way in both:
        one[c, way].start()

    for c in range(2):
        @pl.when(coords[c][0] != 0)
        def _():
            o2[c][0].wait_recv()

    o3 = []
    for c in range(2):
        minor = coords[c][1]
        for k in range(16):
            o3s[c, k] = o2r[c, entry(R_O3 + c, k, 3)]
        old_out[c, pl.ds(2 * minor, 2)] = o3s[c, pl.ds(2 * minor, 2)]
        for step in FAR:
            other, dev = minor_peer(c, step)
            d = copy(o3s.at[c, pl.ds(2 * other, 2)], old_out.at[c, pl.ds(2 * minor, 2)],
                     o3_ss.at[c, step], o3_rs.at[c, step], dev)
            d.start()
            o3.append(d)

    @pl.when(col != 0)
    def _():
        p1[0].wait_recv()

    lower = centred(product(scaled_digits(pan[...]), uinv_out[...]))
    low_out[...] = lower
    top = jnp.where(rank == 0, jnp.where(eye, -1.0, 0.0), lower[:128])
    low_d_out[0] = scaled_digits(top)
    low_d_out[1] = scaled_digits(lower[128:])

    for n in range(2):
        for c, way in both:
            two[c, way, n].wait_recv()
            if n == 0:
                four[c, way].start()
            three[c, way, n].start()

    for d in o3:
        d.wait_recv()
    p2 = []
    for step in range(1, 8):
        p2.append(copy(opan_out, opan_out, p2_ss.at[step], p2_rs, (rank, step)))

    @pl.when(col == 0)
    def _():
        for k in range(16):
            opan_out[k:k + 1, :] = old_out[0, k, 0:1, :]
        for d in p2:
            d.start()

    for d in [*one.values(), *three.values(), *four.values()]:
        d.wait_recv()

    @pl.when(col != 0)
    def _():
        p2[0].wait_recv()

    for c in range(3):
        for k in range(16):
            tab_out[c, k] = first[c, k]
    flag_out[0] = tab[R_OK, 0]

    for d in [*n1, *n2, *o3, *one.values(), *two.values(), *three.values(), *four.values()]:
        d.wait_send()

    @pl.when(rank == 0)
    def _():
        for d in o1:
            d.wait_send()

    for c in range(2):
        @pl.when(coords[c][0] == 0)
        def _():
            for d in o2[c]:
                d.wait_send()

    @pl.when(col == 0)
    def _():
        for d in p1 + p2:
            d.wait_send()


def exchange(pivot_rows, column_order, linv, uinv, mat):
    vmem = pl.BlockSpec(memory_space=pltpu.VMEM)
    smem = pl.BlockSpec(memory_space=pltpu.SMEM)
    dma = pltpu.SemaphoreType.DMA
    tile = lambda *lead: pltpu.VMEM((*lead, 8, 128), F32)
    return pl.pallas_call(
        exchange_kernel,
        name="exchange",
        out_shape=(
            pltpu.VMEM((2, 8, 128, 128), F32),
            pltpu.VMEM((2, 16, 8, 128), F32),
            pltpu.VMEM((16, 128), F32),
            jax.ShapeDtypeStruct((256, 128), F32),
            pltpu.VMEM((2, 256, 256), BF16),
            jax.ShapeDtypeStruct((2, 256, 256), BF16),
            jax.ShapeDtypeStruct((256, 128), BF16),
            pltpu.VMEM((16, 256, 128), F32),
            jax.ShapeDtypeStruct((3, 16), I32),
            jax.ShapeDtypeStruct((1,), I32),
        ),
        in_specs=[vmem] * 4 + [pl.BlockSpec(memory_space=pl.ANY)],
        out_specs=(vmem,) * 8 + (smem, smem),
        scratch_shapes=[
            tile(512), pltpu.VMEM((8, 128), I32), pltpu.SMEM((8, 128), I32),
            pltpu.VMEM((16, 128), I32), pltpu.SMEM((16, 128), I32),
            pltpu.VMEM((256, 128), F32), dma, dma, dma,
            tile(2, 16), tile(2, 16), tile(2, 4), tile(2, 32), tile(2, 128), tile(2, 16),
            tile(2, 32), tile(2, 4), tile(2, 16),
            dma((2, 8)), dma((2, 8)), dma((2, 8)), dma((2, 8)),
            dma((2, 4, 2, 2)), dma((2, 4, 2, 2)),
            dma((2, 8)), dma((2,)), dma((2, 8)), dma((2,)), dma((2, 8)), dma((2, 8)),
            dma((8,)), dma, dma((8,)), dma,
        ],
        compiler_params=pltpu.CompilerParams(
            collective_id=0, has_side_effects=True, vmem_limit_bytes=24 << 20
        ),
    )(pivot_rows.reshape(1, 128), column_order.reshape(1, 128), linv, uinv, mat)


def update_kernel(
    tab, new_ref, old_ref, opan_ref, low_ref, low_d, linv_d, uinv_d, mat, order_ref,
    out_hbm, up_d, out, late, opan, out_sem,
):
    rank, col = lax.axis_index("row"), lax.axis_index("col")
    out2d = out.reshape(257 * 16, 128)
    late2d = late.reshape(256, 128)
    old2d = old_ref.reshape(256, 128)

    def positive(x):
        return jnp.where(x < 0.0, x + PF, x)

    def reduced(x):
        return x - PF * jnp.floor((x + 0.5) * INV)

    first_upper = None
    for pair in range(8):
        c, e = pair // 4, (pair % 4) * 2
        x = jnp.concatenate([new_ref[c, e], new_ref[c, e + 1]], axis=1)
        upper = centred(product(linv_d[c], plain_digits(x)))
        if pair == 0:
            first_upper = upper[:, :128]
        up_d[pair] = plain_digits(upper)

    opan[0:16, :] = opan_ref[...]
    for k in range(16):
        opan[16 + k:17 + k, :] = opan_ref[pl.ds(jnp.clip(tab[2, k], 0, 15), 1), :]
    old_low = centred(product(scaled_digits(opan[...]), uinv_d[...]))
    old_d = [scaled_digits(old_low[:16]), scaled_digits(old_low[16:])]
    for pair in range(8):
        c = pair // 4
        change = product(old_d[c], up_d[pair])
        for side in range(2):
            e = (2 * pair + side) % 8
            value = old2d[pl.ds(128 * c + e, 16, stride=8), :]
            value = reduced(value - change[:, 128 * side:128 * side + 128])
            if pair == 0 and side == 0:
                value = jnp.where(col == 0, positive(old_low[:16]), value)
            late2d[pl.ds(128 * c + e, 16, stride=8), :] = value

    sent = []
    for half in range(2):
        for pair in range(8):
            c = pair // 4
            change = product(low_d[half], up_d[pair])
            for side in range(2):
                e = 2 * pair + side
                value = mat[e, 128 * half:128 * half + 128, :]
                out2d[pl.ds(2048 * half + e, 128, stride=16), :] = reduced(
                    value - change[:, 128 * side:128 * side + 128]
                )
            if pair == 0:
                @pl.when(col == 0)
                def _():
                    part = low_ref[128 * half:128 * half + 128, :]
                    out2d[pl.ds(2048 * half, 128, stride=16), :] = positive(part)

                if half == 0:
                    @pl.when((col == 0) & (rank == 0))
                    def _():
                        sub = lax.broadcasted_iota(I32, (128, 128), 0)
                        order_hot = (sub == order_ref[...]).astype(BF16)
                        out2d[pl.ds(0, 128, stride=16), :] = one_hot_columns(
                            positive(first_upper), order_hot
                        )
            if pair % 4 == 3:
                for k in range(16):
                    slot = tab[c, k]
                    out[jnp.where((slot >> 7) == half, slot, 256), c] = late[c, k]
                where = (pl.ds(128 * half, 128), c)
                d = pltpu.make_async_copy(out.at[where], out_hbm.at[where], out_sem.at[half, c])
                d.start()
                sent.append(d)
    for d in sent:
        d.wait()


def update(tab, new, old, old_panel, low, low_d, linv_d, uinv_d, mat, column_order):
    vmem = pl.BlockSpec(memory_space=pltpu.VMEM)
    return pl.pallas_call(
        update_kernel,
        name="update",
        out_shape=jax.ShapeDtypeStruct((256, 2, 8, 128), F32),
        in_specs=[pl.BlockSpec(memory_space=pltpu.SMEM)] + [vmem] * 9,
        out_specs=pl.BlockSpec(memory_space=pl.ANY),
        scratch_shapes=[
            pltpu.VMEM((8, 256, 256), BF16),
            pltpu.VMEM((257, 2, 8, 128), F32),
            pltpu.VMEM((2, 16, 8, 128), F32),
            pltpu.VMEM((32, 128), F32),
            pltpu.SemaphoreType.DMA((2, 2)),
        ],
        compiler_params=pltpu.CompilerParams(vmem_limit_bytes=24 << 20),
    )(tab, new, old, old_panel, low, low_d, linv_d, uinv_d, mat, column_order.reshape(1, 128))


def on_device(matrix, pivot_rows, column_order, lower_inverse, upper_inverse):
    *parts, tab, flag = exchange(
        pivot_rows, column_order, lower_inverse, upper_inverse, matrix.reshape(512, 8, 128)
    )
    return lax.cond(
        flag[0] > 0,
        lambda: update(tab, *parts, column_order).reshape(matrix.shape),
        lambda: general_path(matrix, pivot_rows, column_order, lower_inverse, upper_inverse),
    )


def solution(mesh):
    return jax.shard_map(
        on_device,
        mesh=mesh,
        in_specs=(P(None, "row", None, "col"), P(), P(), P(), P()),
        out_specs=P(None, "row", None, "col"),
        check_vma=False,
    )
```

```python
import jax
import jax.numpy as jnp
from jax import lax
from jax.experimental import pallas as pl
from jax.experimental.pallas import tpu as pltpu
from jax.sharding import PartitionSpec as P

PF = 32749.0
INV = 1.0 / 32749.0
MESH = pl.DeviceIdType.MESH
F32 = jnp.float32
BF16 = jnp.bfloat16
I32 = jnp.int32


def sum_over(array, axis):
    count = lax.axis_size(axis)
    step = 1
    while step < count:
        array = array + lax.ppermute(array, axis, [(i, i ^ step) for i in range(count)])
        step *= 2
    return array


def general_path(matrix, pivot_rows, column_order, lower_inverse, upper_inverse):
    row_cycles = matrix.shape[0]
    panel_width = matrix.shape[1]
    col_cycles = matrix.shape[2]
    local_rows = row_cycles * panel_width
    local_cols = col_cycles * panel_width
    row_count = lax.axis_size("row")
    row_rank = lax.axis_index("row")
    col_rank = lax.axis_index("col")
    flat = matrix.reshape(local_rows, local_cols)
    stride = row_count * panel_width
    owner = pivot_rows % stride // panel_width
    local_slot = pivot_rows // stride * panel_width + pivot_rows % panel_width
    owned = owner == row_rank
    picked = jnp.where(owned[:, None], flat[jnp.where(owned, local_slot, 0)], 0.0)
    top_rows = jnp.where(row_rank == 0, flat[:panel_width], 0.0)
    new_top, old_top = sum_over(picked, "row"), sum_over(top_rows, "row")
    upper_all = modular_product(lower_inverse.astype(F32), new_top)
    targets = jnp.where(owned, local_slot, local_rows)
    swapped = flat.at[targets].set(old_top, mode="drop")
    panel = swapped[:, :panel_width][:, column_order]
    panel_all = sum_over(jnp.where(col_rank == 0, panel, 0.0), "col")
    lower_all = modular_product(panel_all, upper_inverse.astype(F32))
    permuted = upper_all.at[:, :panel_width].set(upper_all[:, column_order])
    upper_use = jnp.where(col_rank == 0, permuted, upper_all)
    result = swapped - modular_product(lower_all, upper_use)
    result = jnp.where(result < 0.0, result + PF, result)
    result = result.at[:, :panel_width].set(
        jnp.where(col_rank == 0, lower_all, result[:, :panel_width])
    )
    result = result.at[:panel_width].set(jnp.where(row_rank == 0, upper_use, result[:panel_width]))
    return result.reshape(row_cycles, panel_width, col_cycles, panel_width)


def centred(x):
    return x - PF * jnp.floor(x * INV + 0.5)


def scaled_digits(a):
    a = centred(a)
    b = centred(a * 256.0)
    both = jnp.concatenate([b, a], axis=1)
    high = 64.0 * jnp.floor(both * (1.0 / 64.0) + 0.5)
    return jnp.concatenate([high, both - high], axis=0).astype(BF16)


def plain_digits(x):
    high = jnp.floor(x * (1.0 / 256.0))
    return jnp.concatenate([high.astype(BF16), (x - 256.0 * high).astype(BF16)], axis=0)


def product(left, right):
    both = jnp.dot(left, right, preferred_element_type=F32)
    rows = both.shape[0] // 2
    high = both[:rows]
    return (high - (64.0 * PF) * jnp.floor(high * (INV / 64.0))) + both[rows:]


def modular_product(left, right):
    rest = centred(product(scaled_digits(left), plain_digits(right)))
    return jnp.where(rest < 0.0, rest + PF, rest)


def one_hot_columns(values, hot):
    high = jnp.floor(values * (1.0 / 256.0))
    low = values - 256.0 * high
    return 256.0 * jnp.dot(high.astype(BF16), hot, preferred_element_type=F32) + jnp.dot(
        low.astype(BF16), hot, preferred_element_type=F32
    )


R_T2, R_T3, R_O1, R_O2, R_O3, R_OK = 2, 4, 6, 8, 10, 14


def fill_tables(my_z, my_y, pivots_ref, first_ref, out_ref):
    sub = lax.broadcasted_iota(I32, (128, 128), 0)
    lane = lax.broadcasted_iota(I32, (128, 128), 1)
    eye = sub == lane
    t = lax.broadcasted_iota(I32, (1, 128), 1)
    pivots = pivots_ref[...]

    def column(row):
        return jnp.sum(jnp.where(eye, row.astype(F32), 0.0), axis=1, keepdims=True)

    owner = (pivots & 8191) >> 7
    slot_col = column(((pivots >> 13) << 7) | (pivots & 127))
    index_col = lax.broadcasted_iota(I32, (128, 1), 0).astype(F32)
    zero = jnp.zeros((1, 128), I32)
    half, odd = t >> 1, t & 1

    def first(start, residue):
        return start + ((residue - start) & 7)

    halves = []
    for c in range(2):
        if c == 0:
            key, plane, minor = owner, my_z, my_y
        else:
            key, plane, minor = ((owner & 7) << 3) | (owner >> 3), my_y, my_z
        key_col = column(key)
        full_row = (key * 128 + t).astype(F32)
        full_col = key_col * 128.0 + index_col
        rank_col = jnp.sum(jnp.where(full_row < full_col, 1.0, 0.0), axis=1, keepdims=True)

        def before(x, key_col=key_col):
            return jnp.sum(
                jnp.where(key_col < x.astype(F32), 1.0, 0.0), axis=0, keepdims=True
            ).astype(I32)

        def at_rank(values_col, s, rank_col=rank_col):
            return jnp.sum(
                jnp.where(rank_col == s.astype(F32), values_col, 0.0), axis=0, keepdims=True
            ).astype(I32)

        mine = zero + (plane * 8 + minor)
        start = before(mine)
        end = before(mine + 1)
        s = first(start, half) + 8 * odd
        slot = at_rank(slot_col, s)
        held = (s < end) & (t < 16)
        slot = jnp.where(held, slot, -1)
        first_ref[c:c + 1, :] = slot
        if c == 0:
            slot_first = column(slot)
        else:
            same = slot_first == slot.astype(F32)
            place = jnp.sum(jnp.where(same, index_col, 0.0), axis=0, keepdims=True)
            first_ref[2:3, :] = place.astype(I32)
        halves.append((plane, minor, key_col, before, at_rank))

    def rest():
        good = jnp.ones((1, 128), jnp.bool_)
        out_ref[...] = jnp.zeros_like(out_ref)
        for c in range(2):
            good = fill_rest(c, good)
        worst = jnp.min(jnp.where(good, 1.0, 0.0), axis=1, keepdims=True)
        out_ref[R_OK:R_OK + 1, :] = jnp.broadcast_to(worst, (1, 128)).astype(I32)

    def fill_rest(c, good):
        plane, minor, key_col, before, at_rank = halves[c]
        plane_start = before(zero + plane * 8)
        my_first = first(plane_start, minor)
        s = my_first + 8 * t
        key_s = at_rank(key_col, s)
        start = before(key_s)
        where_n2 = (key_s & 7) * 2 + ((s - first(start, minor)) >> 3)
        out_ref[R_T2 + c:R_T2 + c + 1, :] = jnp.clip(where_n2, 0, 15)

        s = 8 * t + minor
        plane_s = at_rank(key_col, s) >> 3
        place = plane_s * 4 + ((s - first(before(plane_s * 8), minor)) >> 3)
        out_ref[R_T3 + c:R_T3 + c + 1, :] = jnp.clip(place, 0, 31)

        s = 8 * (t & 15) + (t >> 4)
        out_ref[R_O1 + c:R_O1 + c + 1, :] = at_rank(index_col, s)

        s = first(before((t >> 2) * 8), minor) + 8 * (t & 3)
        out_ref[R_O2 + c:R_O2 + c + 1, :] = jnp.clip((s - minor) >> 3, 0, 15)

        s = first(before(zero + plane * 8 + half), minor) + 8 * odd
        out_ref[R_O3 + c:R_O3 + c + 1, :] = jnp.clip((s - my_first) >> 3, 0, 3)

        if c == 0:
            good = good & (before(t + 1) - before(t) <= 16)
        good = good & (before(t * 8 + 8) - before(t * 8) <= 32)
        return good

    return rest


FAR = (4, 3, 5, 2, 6, 1, 7)


def exchange_kernel(
    pivots_hbm, order_hbm, linv_hbm, uinv_hbm, mat_hbm,
    new_out, old_out, opan_out, low_out, low_d_out, linv_out, uinv_out, mat_out, tab_out, flag_out,
    pivots_ref, order_ref, linv_ref, uinv_ref, in_sem,
    mat, firstv, first, tabv, tab, pan, mat_sem, first_sem, tab_sem,
    p1s, p1r, p2s, p2r, p3s,
    n1s, n1r, n2s, n2r, o1s, o1r, o2s, o2r, o3s,
    n1_ss, n1_rs, n2_ss, n2_rs, n3_ss, n3_rs, o1_ss, o1_rs, o2_ss, o2_rs, o3_ss, o3_rs,
    p1_ss, p1_rs,
):
    rank = lax.axis_index("row")
    col = lax.axis_index("col")
    z, y = rank // 8, rank % 8
    coords = ((z, y), (y, z))

    def row_of(c, plane, minor):
        return plane * 8 + minor if c == 0 else minor * 8 + plane

    def minor_peer(c, step):
        plane, minor = coords[c]
        other = (minor + step) % 8
        return other, (row_of(c, plane, other), col)

    def plane_peer(c, step):
        plane, minor = coords[c]
        other = (plane + step) % 8
        return other, (row_of(c, other, minor), col)

    def col_peer(step):
        return (rank, (col + step) % 8)

    def copy(src, dst, ssem, rsem, dev):
        return pltpu.make_async_remote_copy(
            src_ref=src, dst_ref=dst, send_sem=ssem, recv_sem=rsem,
            device_id=dev, device_id_type=MESH,
        )

    new2d = new_out.reshape(2 * 8 * 128, 128)

    barrier = pltpu.get_barrier_semaphore()
    for step in range(1, 8):
        for dev in (minor_peer(0, step)[1], minor_peer(1, step)[1], col_peer(step)):
            pl.semaphore_signal(barrier, inc=1, device_id=dev, device_id_type=MESH)

    small = [
        pltpu.make_async_copy(src, dst, in_sem.at[n])
        for n, (src, dst) in enumerate((
            (pivots_hbm, pivots_ref), (order_hbm, order_ref),
            (linv_hbm, linv_ref), (uinv_hbm, uinv_ref),
        ))
    ]
    small[0].start()
    fetch = pltpu.make_async_copy(mat_hbm, mat, mat_sem)
    fetch.start()
    for d in small[1:]:
        d.start()
    small[0].wait()
    fill_rest = fill_tables(z, y, pivots_ref, firstv, tabv)
    to_scalar = pltpu.make_async_copy(firstv, first, first_sem)
    to_scalar.start()
    to_scalar.wait()
    fetch.wait()

    def entry(table, k, top):
        return jnp.clip(tab[table, k], 0, top)

    def mat_tile(row, c):
        return mat[row * 2 + c]

    for c in range(2):
        for k in range(16):
            n1s[c, k] = mat_tile(jnp.clip(first[c, k], 0, 255), c)

    pl.semaphore_wait(barrier, 21)

    n1 = []
    for step in FAR:
        for c in range(2):
            other, dev = minor_peer(c, step)
            minor = coords[c][1]
            d = copy(n1s.at[c, pl.ds(2 * other, 2)], n1r.at[c, pl.ds(2 * minor, 2)],
                     n1_ss.at[c, step], n1_rs.at[c, step], dev)
            d.start()
            n1.append(d)

    fill_rest()
    to_scalar = pltpu.make_async_copy(tabv, tab, tab_sem)
    to_scalar.start()
    to_scalar.wait()

    o1 = []
    for step in FAR:
        for c in range(2):
            dev = (step if c == 0 else step * 8, col)
            o1.append(copy(o1s.at[c, pl.ds(16 * step, 16)], o1r.at[c],
                           o1_ss.at[c, step], o1_rs.at[c], dev))

    @pl.when(rank == 0)
    def _():
        for n, step in enumerate((*FAR, 0)):
            def body(k, carry):
                for c in range(2):
                    o1s[c, 16 * step + k] = mat_tile(entry(R_O1 + c, 16 * step + k, 127), c)
                return carry
            lax.fori_loop(0, 16, body, 0, unroll=4)
            if step:
                o1[2 * n].start()
                o1[2 * n + 1].start()
        for c in range(2):
            o1r[c] = o1s[c, pl.ds(0, 16)]

    p1 = []
    for step in range(1, 8):
        p1.append(copy(pan, pan, p1_ss.at[step], p1_rs, (rank, step)))

    @pl.when(col == 0)
    def _():
        pan[...] = mat.reshape(4096, 128)[pl.ds(0, 256, stride=16), :]
        for d in p1:
            d.start()

    p_one = [copy(p1s.at[pl.ds(16 * step, 16)], p1r, o1_ss.at[2, step], o1_rs.at[2], (step, col))
             for step in FAR]
    p_two = [copy(p2s.at[step], p2r.at[0], o2_ss.at[2, step], o2_rs.at[2],
                  (row_of(0, step, y), col)) for step in FAR]
    p_three = [copy(p3s.at[minor_peer(0, step)[0]], opan_out.at[y], o3_ss.at[2, step],
                    o3_rs.at[2, step], minor_peer(0, step)[1]) for step in FAR]

    for c in range(2):
        minor = coords[c][1]
        n1r[c, pl.ds(2 * minor, 2)] = n1s[c, pl.ds(2 * minor, 2)]

    mat2d = mat.reshape(4096, 128)
    for e in range(16):
        upper_half = mat2d[pl.ds(e, 128, stride=16), :]
        mat_out[e, 0:128, :] = jnp.where(rank == 0, 0.0, upper_half)
        mat_out[e, 128:256, :] = mat2d[pl.ds(2048 + e, 128, stride=16), :]
    for d in small[1:]:
        d.wait()
    sub = lax.broadcasted_iota(I32, (128, 128), 0)
    eye = sub == lax.broadcasted_iota(I32, (128, 128), 1)
    order_hot = (sub == order_ref[...]).astype(BF16)
    uinv = uinv_ref[...].astype(F32)
    u_high = jnp.floor(uinv * (1.0 / 256.0))
    u_low = uinv - 256.0 * u_high
    uperm = 256.0 * jnp.dot(order_hot, u_high.astype(BF16), preferred_element_type=F32) + jnp.dot(
        order_hot, u_low.astype(BF16), preferred_element_type=F32
    )
    uinv_out[...] = plain_digits(centred(uperm))
    linv = linv_ref[...].astype(F32)
    for c in range(2):
        hot = (sub == tabv[R_O1 + c:R_O1 + c + 1, :]).astype(BF16)
        linv_out[c] = scaled_digits(one_hot_columns(linv, hot))

    for d in n1:
        d.wait_recv()

    n2 = []
    for c in range(2):
        plane = coords[c][0]
        for j in range(4):
            row = n1r[c, entry(R_T2 + c, j, 15)]
            n2s[c, j] = row
            n2r[c, plane * 4 + j] = row
    for step in FAR:
        for c in range(2):
            plane = coords[c][0]
            other, dev = plane_peer(c, step)
            d = copy(n2s.at[c], n2r.at[c, pl.ds(4 * plane, 4)],
                     n2_ss.at[c, step], n2_rs.at[c, step], dev)
            d.start()
            n2.append(d)

    @pl.when(col != 0)
    def _():
        p1[0].wait_recv()

    @pl.when(rank == 0)
    def _():
        for k in range(128):
            p1s[k:k + 1, :] = pan[pl.ds(entry(R_O1, k, 127), 1), :]
        for d in p_one:
            d.start()
        p1r[...] = p1s[0:16, :]

    o2 = [[], []]
    for c in range(2):
        plane, minor = coords[c]
        for step in FAR:
            dev = (row_of(c, step, minor), col)
            o2[c].append(copy(o2s.at[c, pl.ds(4 * step, 4)], o2r.at[c],
                              o2_ss.at[c, step], o2_rs.at[c], dev))

    for c in range(2):
        plane, minor = coords[c]

        @pl.when((plane == 0) & (minor != 0))
        def _():
            copy(o1s.at[c, pl.ds(0, 16)], o1r.at[c], o1_ss.at[c, 0], o1_rs.at[c],
                 (0, col)).wait_recv()

        @pl.when(plane == 0)
        def _():
            def body(v, carry):
                o2s[c, v] = o1r[c, entry(R_O2 + c, v, 15)]
                return carry
            lax.fori_loop(0, 32, body, 0)
            for d in o2[c]:
                d.start()
            o2r[c] = o2s[c, pl.ds(0, 4)]

    @pl.when((z == 0) & (y != 0))
    def _():
        p_one[0].wait_recv()

    @pl.when(z == 0)
    def _():
        for v in range(32):
            p2s[v // 4, v % 4:v % 4 + 1, :] = p1r[pl.ds(entry(R_O2, v, 15), 1), :]
        for d in p_two:
            d.start()
        p2r[0] = p2s[0]

    for d in n2:
        d.wait_recv()

    for c in range(2):
        minor = coords[c][1]
        for k in range(16):
            row = n2r[c, entry(R_T3 + c, k, 31)]
            new2d[pl.ds(c * 1024 + minor * 16 + k, 8, stride=128), :] = row

    def part(c, block, e, count):
        rows = pl.ds(pl.multiple_of(16 * block, 16), 16)
        return new_out.at[c, pl.ds(e, count), rows, :]

    def n3_copy(c, kind, way, q, block, e, count, offset):
        piece = part(c, block % 8, e, count)
        return copy(piece, piece, n3_ss.at[c, kind, way, q], n3_rs.at[c, kind, way, q],
                    minor_peer(c, offset)[1])

    both = [(c, way) for c in range(2) for way in range(2)]
    two, one, three, four = {}, {}, {}, {}
    for c, way in both:
        minor = coords[c][1]
        sign = 1 - 2 * way
        one[c, way] = n3_copy(c, 1, way, 0, minor, 0, 8, sign)
        for n in range(2):
            q = n if way == 0 else 1 - n
            two[c, way, n] = n3_copy(c, 0, way, n, minor, 4 * q, 4, 2 * sign)
            three[c, way, n] = n3_copy(c, 2, way, n, minor - 2 * sign, 4 * q, 4, sign)
        four[c, way] = n3_copy(c, 3, way, 0, minor - 2 * sign, 4 * way, 4, 2 * sign)
    for n in range(2):
        for c, way in both:
            two[c, way, n].start()
    for c, way in both:
        one[c, way].start()

    for c in range(2):
        @pl.when(coords[c][0] != 0)
        def _():
            o2[c][0].wait_recv()

    o3 = []
    for c in range(2):
        minor = coords[c][1]
        for k in range(16):
            o3s[c, k] = o2r[c, entry(R_O3 + c, k, 3)]
        old_out[c, pl.ds(2 * minor, 2)] = o3s[c, pl.ds(2 * minor, 2)]
        for step in FAR:
            other, dev = minor_peer(c, step)
            d = copy(o3s.at[c, pl.ds(2 * other, 2)], old_out.at[c, pl.ds(2 * minor, 2)],
                     o3_ss.at[c, step], o3_rs.at[c, step], dev)
            d.start()
            o3.append(d)

    @pl.when(z != 0)
    def _():
        p_two[0].wait_recv()

    for k in range(16):
        p3s[k // 2, k % 2:k % 2 + 1, :] = p2r[0, pl.ds(entry(R_O3, k, 3), 1), :]
    for d in p_three:
        d.start()
    opan_out[y] = p3s[y]

    lower = centred(product(scaled_digits(pan[...]), uinv_out[...]))
    low_out[...] = lower
    top = jnp.where(rank == 0, jnp.where(eye, -1.0, 0.0), lower[:128])
    low_d_out[0] = scaled_digits(top)
    low_d_out[1] = scaled_digits(lower[128:])

    for n in range(2):
        for c, way in both:
            two[c, way, n].wait_recv()
            if n == 0:
                four[c, way].start()
            three[c, way, n].start()

    for d in o3 + p_three:
        d.wait_recv()
    for d in [*one.values(), *three.values(), *four.values()]:
        d.wait_recv()

    for c in range(3):
        for k in range(16):
            tab_out[c, k] = first[c, k]
    flag_out[0] = tab[R_OK, 0]

    for d in [*n1, *n2, *o3, *p_three, *one.values(), *two.values(), *three.values(), *four.values()]:
        d.wait_send()

    @pl.when(rank == 0)
    def _():
        for d in o1 + p_one:
            d.wait_send()

    for c in range(2):
        @pl.when(coords[c][0] == 0)
        def _():
            for d in o2[c] + (p_two if c == 0 else []):
                d.wait_send()

    @pl.when(col == 0)
    def _():
        for d in p1:
            d.wait_send()


def exchange(pivot_rows, column_order, linv, uinv, mat):
    vmem = pl.BlockSpec(memory_space=pltpu.VMEM)
    smem = pl.BlockSpec(memory_space=pltpu.SMEM)
    hbm = pl.BlockSpec(memory_space=pl.ANY)
    dma = pltpu.SemaphoreType.DMA
    tile = lambda *lead: pltpu.VMEM((*lead, 8, 128), F32)
    return pl.pallas_call(
        exchange_kernel,
        name="exchange",
        out_shape=(
            pltpu.VMEM((2, 8, 128, 128), F32),
            pltpu.VMEM((2, 16, 8, 128), F32),
            jax.ShapeDtypeStruct((8, 8, 128), F32),
            jax.ShapeDtypeStruct((256, 128), F32),
            pltpu.VMEM((2, 256, 256), BF16),
            jax.ShapeDtypeStruct((2, 256, 256), BF16),
            jax.ShapeDtypeStruct((256, 128), BF16),
            pltpu.VMEM((16, 256, 128), F32),
            jax.ShapeDtypeStruct((3, 16), I32),
            jax.ShapeDtypeStruct((1,), I32),
        ),
        in_specs=[hbm] * 5,
        out_specs=(vmem,) * 8 + (smem, smem),
        scratch_shapes=[
            pltpu.VMEM((1, 128), I32), pltpu.VMEM((1, 128), I32),
            pltpu.VMEM((128, 128), I32), pltpu.VMEM((128, 128), I32), dma((4,)),
            tile(512), pltpu.VMEM((8, 128), I32), pltpu.SMEM((8, 128), I32),
            pltpu.VMEM((16, 128), I32), pltpu.SMEM((16, 128), I32),
            pltpu.VMEM((256, 128), F32), dma, dma, dma,
            pltpu.VMEM((128, 128), F32), pltpu.VMEM((16, 128), F32), tile(8), tile(1), tile(8),
            tile(2, 16), tile(2, 16), tile(2, 4), tile(2, 32), tile(2, 128), tile(2, 16),
            tile(2, 32), tile(2, 4), tile(2, 16),
            dma((2, 8)), dma((2, 8)), dma((2, 8)), dma((2, 8)),
            dma((2, 4, 2, 2)), dma((2, 4, 2, 2)),
            dma((3, 8)), dma((3,)), dma((3, 8)), dma((3,)), dma((3, 8)), dma((3, 8)),
            dma((8,)), dma,
        ],
        compiler_params=pltpu.CompilerParams(
            collective_id=0, has_side_effects=True, vmem_limit_bytes=24 << 20
        ),
    )(pivot_rows.reshape(1, 128), column_order.reshape(1, 128), linv, uinv, mat)


def update_kernel(
    tab, new_ref, old_ref, opan_ref, low_ref, low_d, linv_d, uinv_d, mat, order_ref,
    out_hbm, up_d, out, late, opan, out_sem,
):
    rank, col = lax.axis_index("row"), lax.axis_index("col")
    out2d = out.reshape(257 * 16, 128)
    late2d = late.reshape(256, 128)
    old2d = old_ref.reshape(256, 128)

    def positive(x):
        return jnp.where(x < 0.0, x + PF, x)

    def reduced(x):
        return x - PF * jnp.floor((x + 0.5) * INV)

    first_upper = None
    for pair in range(8):
        c, e = pair // 4, (pair % 4) * 2
        x = jnp.concatenate([new_ref[c, e], new_ref[c, e + 1]], axis=1)
        upper = centred(product(linv_d[c], plain_digits(x)))
        if pair == 0:
            first_upper = upper[:, :128]
        up_d[pair] = plain_digits(upper)

    for k in range(16):
        opan[k:k + 1, :] = opan_ref[k >> 1, (k & 1):(k & 1) + 1, :]
        there = jnp.clip(tab[2, k], 0, 15)
        opan[16 + k:17 + k, :] = opan_ref[there >> 1, pl.ds(there & 1, 1), :]
    old_low = centred(product(scaled_digits(opan[...]), uinv_d[...]))
    old_d = [scaled_digits(old_low[:16]), scaled_digits(old_low[16:])]
    for pair in range(8):
        c = pair // 4
        change = product(old_d[c], up_d[pair])
        for side in range(2):
            e = (2 * pair + side) % 8
            value = old2d[pl.ds(128 * c + e, 16, stride=8), :]
            value = reduced(value - change[:, 128 * side:128 * side + 128])
            if pair == 0 and side == 0:
                value = jnp.where(col == 0, positive(old_low[:16]), value)
            late2d[pl.ds(128 * c + e, 16, stride=8), :] = value

    sent = []
    for half in range(2):
        for pair in range(8):
            c = pair // 4
            change = product(low_d[half], up_d[pair])
            for side in range(2):
                e = 2 * pair + side
                value = mat[e, 128 * half:128 * half + 128, :]
                out2d[pl.ds(2048 * half + e, 128, stride=16), :] = reduced(
                    value - change[:, 128 * side:128 * side + 128]
                )
            if pair == 0:
                @pl.when(col == 0)
                def _():
                    part = low_ref[128 * half:128 * half + 128, :]
                    out2d[pl.ds(2048 * half, 128, stride=16), :] = positive(part)

                if half == 0:
                    @pl.when((col == 0) & (rank == 0))
                    def _():
                        sub = lax.broadcasted_iota(I32, (128, 128), 0)
                        order_hot = (sub == order_ref[...]).astype(BF16)
                        out2d[pl.ds(0, 128, stride=16), :] = one_hot_columns(
                            positive(first_upper), order_hot
                        )
            if pair % 4 == 3:
                for k in range(16):
                    slot = tab[c, k]
                    out[jnp.where((slot >> 7) == half, slot, 256), c] = late[c, k]
                where = (pl.ds(128 * half, 128), c)
                d = pltpu.make_async_copy(out.at[where], out_hbm.at[where], out_sem.at[half, c])
                d.start()
                sent.append(d)
    for d in sent:
        d.wait()


def update(tab, new, old, old_panel, low, low_d, linv_d, uinv_d, mat, column_order):
    vmem = pl.BlockSpec(memory_space=pltpu.VMEM)
    return pl.pallas_call(
        update_kernel,
        name="update",
        out_shape=jax.ShapeDtypeStruct((256, 2, 8, 128), F32),
        in_specs=[pl.BlockSpec(memory_space=pltpu.SMEM)] + [vmem] * 9,
        out_specs=pl.BlockSpec(memory_space=pl.ANY),
        scratch_shapes=[
            pltpu.VMEM((8, 256, 256), BF16),
            pltpu.VMEM((257, 2, 8, 128), F32),
            pltpu.VMEM((2, 16, 8, 128), F32),
            pltpu.VMEM((32, 128), F32),
            pltpu.SemaphoreType.DMA((2, 2)),
        ],
        compiler_params=pltpu.CompilerParams(vmem_limit_bytes=24 << 20),
    )(tab, new, old, old_panel, low, low_d, linv_d, uinv_d, mat, column_order.reshape(1, 128))


def on_device(matrix, pivot_rows, column_order, lower_inverse, upper_inverse):
    *parts, tab, flag = exchange(
        pivot_rows, column_order, lower_inverse, upper_inverse, matrix.reshape(512, 8, 128)
    )
    return lax.cond(
        flag[0] > 0,
        lambda: update(tab, *parts, column_order).reshape(matrix.shape),
        lambda: general_path(matrix, pivot_rows, column_order, lower_inverse, upper_inverse),
    )


def solution(mesh):
    return jax.shard_map(
        on_device,
        mesh=mesh,
        in_specs=(P(None, "row", None, "col"), P(), P(), P(), P()),
        out_specs=P(None, "row", None, "col"),
        check_vma=False,
    )
```

```python
import jax
import jax.numpy as jnp
from jax import lax
from jax.experimental import pallas as pl
from jax.experimental.pallas import tpu as pltpu
from jax.sharding import PartitionSpec as P

PF = 32749.0
INV = 1.0 / 32749.0
MESH = pl.DeviceIdType.MESH
F32 = jnp.float32
BF16 = jnp.bfloat16
I32 = jnp.int32


def sum_over(array, axis):
    count = lax.axis_size(axis)
    step = 1
    while step < count:
        array = array + lax.ppermute(array, axis, [(i, i ^ step) for i in range(count)])
        step *= 2
    return array


def general_path(matrix, pivot_rows, column_order, lower_inverse, upper_inverse):
    row_cycles = matrix.shape[0]
    panel_width = matrix.shape[1]
    col_cycles = matrix.shape[2]
    local_rows = row_cycles * panel_width
    local_cols = col_cycles * panel_width
    row_count = lax.axis_size("row")
    row_rank = lax.axis_index("row")
    col_rank = lax.axis_index("col")
    flat = matrix.reshape(local_rows, local_cols)
    stride = row_count * panel_width
    owner = pivot_rows % stride // panel_width
    local_slot = pivot_rows // stride * panel_width + pivot_rows % panel_width
    owned = owner == row_rank
    picked = jnp.where(owned[:, None], flat[jnp.where(owned, local_slot, 0)], 0.0)
    top_rows = jnp.where(row_rank == 0, flat[:panel_width], 0.0)
    new_top, old_top = sum_over(picked, "row"), sum_over(top_rows, "row")
    upper_all = modular_product(lower_inverse.astype(F32), new_top)
    targets = jnp.where(owned, local_slot, local_rows)
    swapped = flat.at[targets].set(old_top, mode="drop")
    panel = swapped[:, :panel_width][:, column_order]
    panel_all = sum_over(jnp.where(col_rank == 0, panel, 0.0), "col")
    lower_all = modular_product(panel_all, upper_inverse.astype(F32))
    permuted = upper_all.at[:, :panel_width].set(upper_all[:, column_order])
    upper_use = jnp.where(col_rank == 0, permuted, upper_all)
    result = swapped - modular_product(lower_all, upper_use)
    result = jnp.where(result < 0.0, result + PF, result)
    result = result.at[:, :panel_width].set(
        jnp.where(col_rank == 0, lower_all, result[:, :panel_width])
    )
    result = result.at[:panel_width].set(jnp.where(row_rank == 0, upper_use, result[:panel_width]))
    return result.reshape(row_cycles, panel_width, col_cycles, panel_width)


def centred(x):
    return x - PF * jnp.floor(x * INV + 0.5)


def scaled_digits(a):
    a = centred(a)
    b = centred(a * 256.0)
    both = jnp.concatenate([b, a], axis=1)
    high = 64.0 * jnp.floor(both * (1.0 / 64.0) + 0.5)
    return jnp.concatenate([high, both - high], axis=0).astype(BF16)


def plain_digits(x):
    high = jnp.floor(x * (1.0 / 256.0))
    return jnp.concatenate([high.astype(BF16), (x - 256.0 * high).astype(BF16)], axis=0)


def product(left, right):
    both = jnp.dot(left, right, preferred_element_type=F32)
    rows = both.shape[0] // 2
    high = both[:rows]
    return (high - (64.0 * PF) * jnp.floor(high * (INV / 64.0))) + both[rows:]


def modular_product(left, right):
    rest = centred(product(scaled_digits(left), plain_digits(right)))
    return jnp.where(rest < 0.0, rest + PF, rest)


def one_hot_columns(values, hot):
    high = jnp.floor(values * (1.0 / 256.0))
    low = values - 256.0 * high
    return 256.0 * jnp.dot(high.astype(BF16), hot, preferred_element_type=F32) + jnp.dot(
        low.astype(BF16), hot, preferred_element_type=F32
    )


R_T2, R_T3, R_O1, R_O2, R_O3, R_OK = 2, 4, 6, 8, 10, 14


def fill_tables(my_z, my_y, pivots_ref, first_ref, out_ref):
    sub = lax.broadcasted_iota(I32, (128, 128), 0)
    lane = lax.broadcasted_iota(I32, (128, 128), 1)
    eye = sub == lane
    t = lax.broadcasted_iota(I32, (1, 128), 1)
    pivots = pivots_ref[...]

    def column(row):
        return jnp.sum(jnp.where(eye, row.astype(F32), 0.0), axis=1, keepdims=True)

    owner = (pivots & 8191) >> 7
    slot_col = column(((pivots >> 13) << 7) | (pivots & 127))
    index_col = lax.broadcasted_iota(I32, (128, 1), 0).astype(F32)
    zero = jnp.zeros((1, 128), I32)
    half, odd = t >> 1, t & 1

    def first(start, residue):
        return start + ((residue - start) & 7)

    halves = []
    for c in range(2):
        if c == 0:
            key, plane, minor = owner, my_z, my_y
        else:
            key, plane, minor = ((owner & 7) << 3) | (owner >> 3), my_y, my_z
        key_col = column(key)
        full_row = (key * 128 + t).astype(F32)
        full_col = key_col * 128.0 + index_col
        rank_col = jnp.sum(jnp.where(full_row < full_col, 1.0, 0.0), axis=1, keepdims=True)

        def before(x, key_col=key_col):
            return jnp.sum(
                jnp.where(key_col < x.astype(F32), 1.0, 0.0), axis=0, keepdims=True
            ).astype(I32)

        def at_rank(values_col, s, rank_col=rank_col):
            return jnp.sum(
                jnp.where(rank_col == s.astype(F32), values_col, 0.0), axis=0, keepdims=True
            ).astype(I32)

        mine = zero + (plane * 8 + minor)
        start = before(mine)
        end = before(mine + 1)
        s = first(start, half) + 8 * odd
        slot = at_rank(slot_col, s)
        held = (s < end) & (t < 16)
        slot = jnp.where(held, slot, -1)
        first_ref[c:c + 1, :] = slot
        if c == 0:
            slot_first = column(slot)
        else:
            same = slot_first == slot.astype(F32)
            place = jnp.sum(jnp.where(same, index_col, 0.0), axis=0, keepdims=True)
            first_ref[2:3, :] = place.astype(I32)
        halves.append((plane, minor, key_col, before, at_rank))

    def rest():
        good = jnp.ones((1, 128), jnp.bool_)
        out_ref[...] = jnp.zeros_like(out_ref)
        for c in range(2):
            good = fill_rest(c, good)
        worst = jnp.min(jnp.where(good, 1.0, 0.0), axis=1, keepdims=True)
        out_ref[R_OK:R_OK + 1, :] = jnp.broadcast_to(worst, (1, 128)).astype(I32)

    def fill_rest(c, good):
        plane, minor, key_col, before, at_rank = halves[c]
        plane_start = before(zero + plane * 8)
        my_first = first(plane_start, minor)
        s = my_first + 8 * t
        key_s = at_rank(key_col, s)
        start = before(key_s)
        where_n2 = (key_s & 7) * 2 + ((s - first(start, minor)) >> 3)
        out_ref[R_T2 + c:R_T2 + c + 1, :] = jnp.clip(where_n2, 0, 15)

        s = 8 * t + minor
        plane_s = at_rank(key_col, s) >> 3
        place = plane_s * 4 + ((s - first(before(plane_s * 8), minor)) >> 3)
        out_ref[R_T3 + c:R_T3 + c + 1, :] = jnp.clip(place, 0, 31)

        s = 8 * (t & 15) + (t >> 4)
        out_ref[R_O1 + c:R_O1 + c + 1, :] = at_rank(index_col, s)

        s = first(before((t >> 2) * 8), minor) + 8 * (t & 3)
        out_ref[R_O2 + c:R_O2 + c + 1, :] = jnp.clip((s - minor) >> 3, 0, 15)

        s = first(before(zero + plane * 8 + half), minor) + 8 * odd
        out_ref[R_O3 + c:R_O3 + c + 1, :] = jnp.clip((s - my_first) >> 3, 0, 3)

        if c == 0:
            good = good & (before(t + 1) - before(t) <= 16)
        good = good & (before(t * 8 + 8) - before(t * 8) <= 32)
        return good

    return rest


FAR = (4, 3, 5, 2, 6, 1, 7)


def exchange_kernel(
    pivots_hbm, order_hbm, linv_hbm, uinv_hbm, mat_hbm,
    new_out, old_out, opan_out, low_out, low_d_out, linv_out, uinv_out, mat_out, tab_out, flag_out,
    pivots_ref, order_ref, linv_ref, uinv_ref, in_sem,
    mat, firstv, first, tabv, tab, pan, mat_sem, first_sem, tab_sem,
    p1s, p1r, p2s, p2r, p3s,
    n1s, n1r, n2s, n2r, o1s, o1r, o2s, o2r, o3s,
    n1_ss, n1_rs, n2_ss, n2_rs, n3_ss, n3_rs, o1_ss, o1_rs, o2_ss, o2_rs, o3_ss, o3_rs,
    p1_ss, p1_rs,
):
    rank = lax.axis_index("row")
    col = lax.axis_index("col")
    z, y = rank // 8, rank % 8
    coords = ((z, y), (y, z))

    def row_of(c, plane, minor):
        return plane * 8 + minor if c == 0 else minor * 8 + plane

    def minor_peer(c, step):
        plane, minor = coords[c]
        other = (minor + step) % 8
        return other, (row_of(c, plane, other), col)

    def plane_peer(c, step):
        plane, minor = coords[c]
        other = (plane + step) % 8
        return other, (row_of(c, other, minor), col)

    def col_peer(step):
        return (rank, (col + step) % 8)

    def copy(src, dst, ssem, rsem, dev):
        return pltpu.make_async_remote_copy(
            src_ref=src, dst_ref=dst, send_sem=ssem, recv_sem=rsem,
            device_id=dev, device_id_type=MESH,
        )

    new2d = new_out.reshape(2 * 8 * 128, 128)

    barrier = pltpu.get_barrier_semaphore()
    for step in range(1, 8):
        for dev in (minor_peer(0, step)[1], minor_peer(1, step)[1], col_peer(step)):
            pl.semaphore_signal(barrier, inc=1, device_id=dev, device_id_type=MESH)

    small = [
        pltpu.make_async_copy(src, dst, in_sem.at[n])
        for n, (src, dst) in enumerate((
            (pivots_hbm, pivots_ref), (order_hbm, order_ref),
            (linv_hbm, linv_ref), (uinv_hbm, uinv_ref),
        ))
    ]
    small[0].start()
    fetch = pltpu.make_async_copy(mat_hbm, mat, mat_sem)
    fetch.start()
    for d in small[1:]:
        d.start()
    small[0].wait()
    fill_rest = fill_tables(z, y, pivots_ref, firstv, tabv)
    to_scalar = pltpu.make_async_copy(firstv, first, first_sem)
    to_scalar.start()
    to_scalar.wait()
    fetch.wait()

    def entry(table, k, top):
        return jnp.clip(tab[table, k], 0, top)

    def mat_tile(row, c):
        return mat[row * 2 + c]

    for c in range(2):
        for k in range(16):
            n1s[c, k] = mat_tile(jnp.clip(first[c, k], 0, 255), c)

    pl.semaphore_wait(barrier, 21)

    n1 = []
    for step in FAR:
        for c in range(2):
            other, dev = minor_peer(c, step)
            minor = coords[c][1]
            d = copy(n1s.at[c, pl.ds(2 * other, 2)], n1r.at[c, pl.ds(2 * minor, 2)],
                     n1_ss.at[c, step], n1_rs.at[c, step], dev)
            d.start()
            n1.append(d)

    fill_rest()
    to_scalar = pltpu.make_async_copy(tabv, tab, tab_sem)
    to_scalar.start()
    to_scalar.wait()

    o1 = []
    for step in FAR:
        for c in range(2):
            dev = (step if c == 0 else step * 8, col)
            o1.append(copy(o1s.at[c, pl.ds(16 * step, 16)], o1r.at[c],
                           o1_ss.at[c, step], o1_rs.at[c], dev))

    @pl.when(rank == 0)
    def _():
        for n, step in enumerate((*FAR, 0)):
            def body(k, carry):
                for c in range(2):
                    o1s[c, 16 * step + k] = mat_tile(entry(R_O1 + c, 16 * step + k, 127), c)
                return carry
            lax.fori_loop(0, 16, body, 0, unroll=4)
            if step:
                o1[2 * n].start()
                o1[2 * n + 1].start()
        for c in range(2):
            o1r[c] = o1s[c, pl.ds(0, 16)]

    p1 = []
    for step in range(1, 8):
        p1.append(copy(pan, pan, p1_ss.at[step], p1_rs, (rank, step)))

    @pl.when(col == 0)
    def _():
        pan[...] = mat.reshape(4096, 128)[pl.ds(0, 256, stride=16), :]
        for d in p1:
            d.start()

    p_one = [copy(p1s.at[pl.ds(16 * step, 16)], p1r, o1_ss.at[2, step], o1_rs.at[2], (step, col))
             for step in FAR]
    p_two = [copy(p2s.at[step], p2r.at[0], o2_ss.at[2, step], o2_rs.at[2],
                  (row_of(0, step, y), col)) for step in FAR]
    p_three = [copy(p3s.at[minor_peer(0, step)[0]], opan_out.at[y], o3_ss.at[2, step],
                    o3_rs.at[2, step], minor_peer(0, step)[1]) for step in FAR]

    for c in range(2):
        minor = coords[c][1]
        n1r[c, pl.ds(2 * minor, 2)] = n1s[c, pl.ds(2 * minor, 2)]

    mat2d = mat.reshape(4096, 128)
    for e in range(16):
        upper_half = mat2d[pl.ds(e, 128, stride=16), :]
        mat_out[e, 0:128, :] = jnp.where(rank == 0, 0.0, upper_half)
        mat_out[e, 128:256, :] = mat2d[pl.ds(2048 + e, 128, stride=16), :]
    for d in small[1:]:
        d.wait()
    sub = lax.broadcasted_iota(I32, (128, 128), 0)
    eye = sub == lax.broadcasted_iota(I32, (128, 128), 1)
    order_hot = (sub == order_ref[...]).astype(BF16)
    uinv = uinv_ref[...].astype(F32)
    u_high = jnp.floor(uinv * (1.0 / 256.0))
    u_low = uinv - 256.0 * u_high
    uperm = 256.0 * jnp.dot(order_hot, u_high.astype(BF16), preferred_element_type=F32) + jnp.dot(
        order_hot, u_low.astype(BF16), preferred_element_type=F32
    )
    uinv_out[...] = plain_digits(centred(uperm))
    linv = linv_ref[...].astype(F32)
    for c in range(2):
        hot = (sub == tabv[R_O1 + c:R_O1 + c + 1, :]).astype(BF16)
        linv_out[c] = scaled_digits(one_hot_columns(linv, hot))

    for d in n1:
        d.wait_recv()

    n2 = []
    for c in range(2):
        plane = coords[c][0]
        for j in range(4):
            row = n1r[c, entry(R_T2 + c, j, 15)]
            n2s[c, j] = row
            n2r[c, plane * 4 + j] = row
    for step in FAR:
        for c in range(2):
            plane = coords[c][0]
            other, dev = plane_peer(c, step)
            d = copy(n2s.at[c], n2r.at[c, pl.ds(4 * plane, 4)],
                     n2_ss.at[c, step], n2_rs.at[c, step], dev)
            d.start()
            n2.append(d)

    @pl.when(col != 0)
    def _():
        p1[0].wait_recv()

    @pl.when(rank == 0)
    def _():
        for k in range(128):
            p1s[k:k + 1, :] = pan[pl.ds(entry(R_O1, k, 127), 1), :]
        for d in p_one:
            d.start()
        p1r[...] = p1s[0:16, :]

    o2 = [[], []]
    for c in range(2):
        plane, minor = coords[c]
        for step in FAR:
            dev = (row_of(c, step, minor), col)
            o2[c].append(copy(o2s.at[c, pl.ds(4 * step, 4)], o2r.at[c],
                              o2_ss.at[c, step], o2_rs.at[c], dev))

    for c in range(2):
        plane, minor = coords[c]

        @pl.when((plane == 0) & (minor != 0))
        def _():
            copy(o1s.at[c, pl.ds(0, 16)], o1r.at[c], o1_ss.at[c, 0], o1_rs.at[c],
                 (0, col)).wait_recv()

        @pl.when(plane == 0)
        def _():
            def body(v, carry):
                o2s[c, v] = o1r[c, entry(R_O2 + c, v, 15)]
                return carry
            lax.fori_loop(0, 32, body, 0)
            for d in o2[c]:
                d.start()
            o2r[c] = o2s[c, pl.ds(0, 4)]

    @pl.when((z == 0) & (y != 0))
    def _():
        p_one[0].wait_recv()

    @pl.when(z == 0)
    def _():
        for v in range(32):
            p2s[v // 4, v % 4:v % 4 + 1, :] = p1r[pl.ds(entry(R_O2, v, 15), 1), :]
        for d in p_two:
            d.start()
        p2r[0] = p2s[0]

    for d in n2:
        d.wait_recv()

    for c in range(2):
        minor = coords[c][1]
        for k in range(16):
            row = n2r[c, entry(R_T3 + c, k, 31)]
            new2d[pl.ds(c * 1024 + minor * 16 + k, 8, stride=128), :] = row

    def part(c, block, e, count):
        rows = pl.ds(pl.multiple_of(16 * block, 16), 16)
        return new_out.at[c, pl.ds(e, count), rows, :]

    def n3_copy(c, kind, way, q, block, e, count, offset):
        piece = part(c, block % 8, e, count)
        return copy(piece, piece, n3_ss.at[c, kind, way, q], n3_rs.at[c, kind, way, q],
                    minor_peer(c, offset)[1])

    both = [(c, way) for c in range(2) for way in range(2)]
    two, one, three, four = {}, {}, {}, {}
    for c, way in both:
        minor = coords[c][1]
        sign = 1 - 2 * way
        one[c, way] = n3_copy(c, 1, way, 0, minor, 0, 8, sign)
        for n in range(2):
            q = n if way == 0 else 1 - n
            two[c, way, n] = n3_copy(c, 0, way, n, minor, 4 * q, 4, 2 * sign)
            three[c, way, n] = n3_copy(c, 2, way, n, minor - 2 * sign, 4 * q, 4, sign)
        four[c, way] = n3_copy(c, 3, way, 0, minor - 2 * sign, 4 * way, 4, 2 * sign)
    for n in range(2):
        for c, way in both:
            two[c, way, n].start()
    for c, way in both:
        one[c, way].start()

    for c in range(2):
        @pl.when(coords[c][0] != 0)
        def _():
            o2[c][0].wait_recv()

    o3 = []
    for c in range(2):
        minor = coords[c][1]
        for k in range(16):
            o3s[c, k] = o2r[c, entry(R_O3 + c, k, 3)]
        old_out[c, pl.ds(2 * minor, 2)] = o3s[c, pl.ds(2 * minor, 2)]
        for step in FAR:
            other, dev = minor_peer(c, step)
            d = copy(o3s.at[c, pl.ds(2 * other, 2)], old_out.at[c, pl.ds(2 * minor, 2)],
                     o3_ss.at[c, step], o3_rs.at[c, step], dev)
            d.start()
            o3.append(d)

    @pl.when(z != 0)
    def _():
        p_two[0].wait_recv()

    for k in range(16):
        p3s[k // 2, k % 2:k % 2 + 1, :] = p2r[0, pl.ds(entry(R_O3, k, 3), 1), :]
    for d in p_three:
        d.start()
    opan_out[y] = p3s[y]

    lower = centred(product(scaled_digits(pan[...]), uinv_out[...]))
    low_out[...] = lower
    top = jnp.where(rank == 0, jnp.where(eye, -1.0, 0.0), lower[:128])
    low_d_out[0] = scaled_digits(top)
    low_d_out[1] = scaled_digits(lower[128:])

    for n in range(2):
        for c, way in both:
            two[c, way, n].wait_recv()
            if n == 0:
                four[c, way].start()
            three[c, way, n].start()

    for d in o3 + p_three:
        d.wait_recv()
    for d in [*one.values(), *three.values(), *four.values()]:
        d.wait_recv()

    for c in range(3):
        for k in range(16):
            tab_out[c, k] = first[c, k]
    flag_out[0] = tab[R_OK, 0]

    for d in [*n1, *n2, *o3, *p_three, *one.values(), *two.values(), *three.values(), *four.values()]:
        d.wait_send()

    @pl.when(rank == 0)
    def _():
        for d in o1 + p_one:
            d.wait_send()

    for c in range(2):
        @pl.when(coords[c][0] == 0)
        def _():
            for d in o2[c] + (p_two if c == 0 else []):
                d.wait_send()

    @pl.when(col == 0)
    def _():
        for d in p1:
            d.wait_send()


def exchange(pivot_rows, column_order, linv, uinv, mat):
    vmem = pl.BlockSpec(memory_space=pltpu.VMEM)
    smem = pl.BlockSpec(memory_space=pltpu.SMEM)
    hbm = pl.BlockSpec(memory_space=pl.ANY)
    dma = pltpu.SemaphoreType.DMA
    tile = lambda *lead: pltpu.VMEM((*lead, 8, 128), F32)
    return pl.pallas_call(
        exchange_kernel,
        name="exchange",
        out_shape=(
            pltpu.VMEM((2, 8, 128, 128), F32),
            pltpu.VMEM((2, 16, 8, 128), F32),
            jax.ShapeDtypeStruct((8, 8, 128), F32),
            jax.ShapeDtypeStruct((256, 128), F32),
            pltpu.VMEM((2, 256, 256), BF16),
            jax.ShapeDtypeStruct((2, 256, 256), BF16),
            jax.ShapeDtypeStruct((256, 128), BF16),
            pltpu.VMEM((16, 256, 128), F32),
            jax.ShapeDtypeStruct((3, 16), I32),
            jax.ShapeDtypeStruct((1,), I32),
        ),
        in_specs=[hbm] * 5,
        out_specs=(vmem,) * 8 + (smem, smem),
        scratch_shapes=[
            pltpu.VMEM((1, 128), I32), pltpu.VMEM((1, 128), I32),
            pltpu.VMEM((128, 128), I32), pltpu.VMEM((128, 128), I32), dma((4,)),
            tile(512), pltpu.VMEM((8, 128), I32), pltpu.SMEM((8, 128), I32),
            pltpu.VMEM((16, 128), I32), pltpu.SMEM((16, 128), I32),
            pltpu.VMEM((256, 128), F32), dma, dma, dma,
            pltpu.VMEM((128, 128), F32), pltpu.VMEM((16, 128), F32), tile(8), tile(1), tile(8),
            tile(2, 16), tile(2, 16), tile(2, 4), tile(2, 32), tile(2, 128), tile(2, 16),
            tile(2, 32), tile(2, 4), tile(2, 16),
            dma((2, 8)), dma((2, 8)), dma((2, 8)), dma((2, 8)),
            dma((2, 4, 2, 2)), dma((2, 4, 2, 2)),
            dma((3, 8)), dma((3,)), dma((3, 8)), dma((3,)), dma((3, 8)), dma((3, 8)),
            dma((8,)), dma,
        ],
        compiler_params=pltpu.CompilerParams(
            collective_id=0, has_side_effects=True, vmem_limit_bytes=24 << 20
        ),
    )(pivot_rows.reshape(1, 128), column_order.reshape(1, 128), linv, uinv, mat)


def update_kernel(
    tab, new_ref, old_ref, opan_ref, low_ref, low_d, linv_d, uinv_d, mat, order_ref,
    out_hbm, up_d, out, late, opan, out_sem,
):
    rank, col = lax.axis_index("row"), lax.axis_index("col")
    out2d = out.reshape(257 * 16, 128)
    late2d = late.reshape(256, 128)
    old2d = old_ref.reshape(256, 128)

    def positive(x):
        return jnp.where(x < 0.0, x + PF, x)

    def reduced(x):
        return x - PF * jnp.floor((x + 0.5) * INV)

    def make_upper(pair):
        c, e = pair // 4, (pair % 4) * 2
        x = jnp.concatenate([new_ref[c, e], new_ref[c, e + 1]], axis=1)
        upper = centred(product(linv_d[c], plain_digits(x)))
        up_d[pair] = plain_digits(upper)
        return upper

    def finish(pair, half, change):
        for side in range(2):
            e = 2 * pair + side
            value = mat[e, 128 * half:128 * half + 128, :]
            out2d[pl.ds(2048 * half + e, 128, stride=16), :] = reduced(
                value - change[:, 128 * side:128 * side + 128]
            )

    for k in range(16):
        opan[k:k + 1, :] = opan_ref[k >> 1, (k & 1):(k & 1) + 1, :]
        there = jnp.clip(tab[2, k], 0, 15)
        opan[16 + k:17 + k, :] = opan_ref[there >> 1, pl.ds(there & 1, 1), :]
    old_low = centred(product(scaled_digits(opan[...]), uinv_d[...]))
    old_d = [scaled_digits(old_low[:16]), scaled_digits(old_low[16:])]

    def displaced(pair):
        c = pair // 4
        change = product(old_d[c], up_d[pair])
        for side in range(2):
            e = (2 * pair + side) % 8
            value = old2d[pl.ds(128 * c + e, 16, stride=8), :]
            value = reduced(value - change[:, 128 * side:128 * side + 128])
            if pair == 0 and side == 0:
                value = jnp.where(col == 0, positive(old_low[:16]), value)
            late2d[pl.ds(128 * c + e, 16, stride=8), :] = value

    first_upper = make_upper(0)[:, :128]
    for pair in range(1, 4):
        make_upper(pair)
    for pair in range(4):
        make_upper(4 + pair)
        displaced(pair)
        for half in range(2):
            finish(pair, half, product(low_d[half], up_d[pair]))
    for pair in range(4, 8):
        displaced(pair)

    @pl.when(col == 0)
    def _():
        out2d[pl.ds(0, 256, stride=16), :] = positive(low_ref[...])

        @pl.when(rank == 0)
        def _():
            sub = lax.broadcasted_iota(I32, (128, 128), 0)
            order_hot = (sub == order_ref[...]).astype(BF16)
            out2d[pl.ds(0, 128, stride=16), :] = one_hot_columns(positive(first_upper), order_hot)

    sent = []

    def send(half, c):
        for k in range(16):
            slot = tab[c, k]
            out[jnp.where((slot >> 7) == half, slot, 256), c] = late[c, k]
        where = (pl.ds(128 * half, 128), c)
        d = pltpu.make_async_copy(out.at[where], out_hbm.at[where], out_sem.at[half, c])
        d.start()
        sent.append(d)

    send(0, 0)
    send(1, 0)
    for half in range(2):
        for pair in range(4, 8):
            finish(pair, half, product(low_d[half], up_d[pair]))
        send(half, 1)
    for d in sent:
        d.wait()


def update(tab, new, old, old_panel, low, low_d, linv_d, uinv_d, mat, column_order):
    vmem = pl.BlockSpec(memory_space=pltpu.VMEM)
    return pl.pallas_call(
        update_kernel,
        name="update",
        out_shape=jax.ShapeDtypeStruct((256, 2, 8, 128), F32),
        in_specs=[pl.BlockSpec(memory_space=pltpu.SMEM)] + [vmem] * 9,
        out_specs=pl.BlockSpec(memory_space=pl.ANY),
        scratch_shapes=[
            pltpu.VMEM((8, 256, 256), BF16),
            pltpu.VMEM((257, 2, 8, 128), F32),
            pltpu.VMEM((2, 16, 8, 128), F32),
            pltpu.VMEM((32, 128), F32),
            pltpu.SemaphoreType.DMA((2, 2)),
        ],
        compiler_params=pltpu.CompilerParams(vmem_limit_bytes=24 << 20),
    )(tab, new, old, old_panel, low, low_d, linv_d, uinv_d, mat, column_order.reshape(1, 128))


def on_device(matrix, pivot_rows, column_order, lower_inverse, upper_inverse):
    *parts, tab, flag = exchange(
        pivot_rows, column_order, lower_inverse, upper_inverse, matrix.reshape(512, 8, 128)
    )
    return lax.cond(
        flag[0] > 0,
        lambda: update(tab, *parts, column_order).reshape(matrix.shape),
        lambda: general_path(matrix, pivot_rows, column_order, lower_inverse, upper_inverse),
    )


def solution(mesh):
    return jax.shard_map(
        on_device,
        mesh=mesh,
        in_specs=(P(None, "row", None, "col"), P(), P(), P(), P()),
        out_specs=P(None, "row", None, "col"),
        check_vma=False,
    )
```
